256 devices in a mesh: aux: 8 (over y, core), row: 32 (over x, z).
Axes of the slice: x: 4, y: 4, z: 8, core: 2. Of those that a mesh axis runs over, the one named last changes fastest.
Arguments:
- integrals: bfloat16 [32, 64, 4, 256, 256], P('aux', 'row'), may hold values from -6 to 6
- block_columns: int32 [64, 4], P('row'), may hold values from 0 to 63, as said below
- orbitals: bfloat16 [16384, 2048], P('row'), may hold values from -0.1875 to 0.1875
- occ_mask: int32 [64, 32], replicated, may hold values from 0 to 1, as said below
Outputs:
- exchange: float32 [16384, 1536], P('row', 'aux')
The draws below stay inside these ranges and needn't reach their ends.
Inputs may be any that keep to these rules, and one draw needn't show every extreme that they name: `block_columns`: each row block has 4 different column blocks, each lying on the same row device as the row block or on the one beside it. `occ_mask`: entry (b, s) is 1 when row block b lies on row device s, and 0 when it lies on a device more than one away from s.
All inputs are finite; a program needn't handle non-finite values.
Results may differ from the reference program's by a relative error of at most 0.0018.
Values may be sent and summed in bfloat16 or wider, within the bound.
No kernel may reach another device: no remote copies, remote signals or barrier semaphores. Data moves between devices by JAX's collectives and lax.ppermute only.
A program may use at most 128 MiB of HBM per device.

```python
import jax
import jax.numpy as jnp
from jax import lax

MU_DEV = 512
BS = 256
KEPT = 4
NOCC = 2048
NAUX = 32
NBF = 16384
RB = 2
NB = 64
OB = 64
N_ROW = 32


def draw_block_columns(key, part):
    scores = jax.random.randint(key, (NB, 3 * RB), 0, 1 << 20)
    scores = scores * (3 * RB) + jnp.arange(3 * RB, dtype=jnp.int32)[None, :]
    device = jnp.arange(NB, dtype=jnp.int32) // RB
    column = (device[:, None] - 1) * RB + jnp.arange(3 * RB, dtype=jnp.int32)[None, :]
    usable = (column >= 0) & (column < NB)
    scores = jnp.where(usable, scores, scores + (1 << 28))
    ranked = jnp.argsort(scores, axis=1, stable=True)[:, :KEPT]
    return jnp.take_along_axis(column, ranked, axis=1).astype(jnp.int32)


def draw_occ_mask(key, part):
    tosses = jax.random.randint(key, (NB, N_ROW), 0, 4)
    owners = jnp.arange(NB, dtype=jnp.int32)[:, None] // RB
    slices = jnp.arange(N_ROW, dtype=jnp.int32)[None, :]
    distance = jnp.abs(owners - slices)
    nearby = jnp.where(tosses > 0, 1, 0)
    return jnp.where(distance == 0, 1, jnp.where(distance == 1, nearby, 0)).astype(jnp.int32)


def level_of(own_key, extent, pieces, low, top_value):
    loudness = 1.0
    for position, blocks in pieces:
        draws = jax.random.uniform(jax.random.fold_in(jax.random.fold_in(own_key, 6), position), (blocks,), jnp.float32, low / len(pieces), top_value / len(pieces))
        loudness = loudness * jnp.repeat(jnp.exp(draws), extent[position] // blocks).reshape((-1,) + (1,) * (len(extent) - 1 - position))
    return loudness


def scatter_about(rng, shape, deviation, reach, split=(), kind=jnp.bfloat16):
    level = level_of(rng, shape, split, -0.22, 0.18) if split else 1.0
    array = jax.random.normal(rng, shape, jnp.float32) * deviation * level
    return jnp.minimum(jnp.maximum(array, -reach), reach).astype(kind)


def setup_inputs(seed: int = 0) -> dict:
    streams_of = jax.random.split(jax.random.key(seed), 5)
    return {
        "integrals": scatter_about(streams_of[0], (NAUX, NB, KEPT, BS, BS), 1.0, 6.0, ((0, 8), (1, 32))),
        "block_columns": draw_block_columns(jax.random.fold_in(streams_of[4], 71), 0),
        "orbitals": scatter_about(streams_of[2], (NBF, NOCC), (KEPT * BS) ** -0.5, 0.1875, ((0, 32),)),
        "occ_mask": draw_occ_mask(jax.random.fold_in(streams_of[4], 71), 0),
    }


def reference(integrals, block_columns, orbitals, occ_mask):
    weight_scale = 1.0 / (NAUX * OB) ** 0.5
    orbital_blocks = orbitals.reshape(NB, BS, NOCC)

    def window_half(source):
        occupied = lax.dynamic_slice_in_dim(orbital_blocks, source * OB, OB, 2)
        stacked = []
        for place in range(3):
            neighbor = source - 1 + place
            inside = ((neighbor >= 0) & (neighbor < N_ROW)).astype(jnp.float32)
            clipped = jnp.clip(neighbor, 0, N_ROW - 1).astype(jnp.int32)
            blocks = lax.dynamic_slice_in_dim(integrals, clipped * RB, RB, 1)
            columns = lax.dynamic_slice_in_dim(block_columns, clipped * RB, RB, 0)
            picked = occupied[columns]
            half = jnp.einsum('prkml,rklj->pjrm', blocks.astype(jnp.float32), picked.astype(jnp.float32))
            mask_rows = lax.dynamic_slice_in_dim(occ_mask, clipped * RB, RB, 0)
            factor = lax.dynamic_slice_in_dim(mask_rows, source, 1, 1)[:, 0].astype(jnp.float32) * inside
            half = half * factor[None, None, :, None]
            stacked.append(half.reshape(NAUX, OB, MU_DEV))
        return jnp.concatenate(stacked, 2).astype(jnp.bfloat16)

    windows = lax.map(window_half, jnp.arange(N_ROW, dtype=jnp.int32))

    def owner_rows(owner):
        summed = jnp.zeros((MU_DEV, 3 * MU_DEV), jnp.float32)
        for place in range(3):
            source = owner + 1 - place
            inside = ((source >= 0) & (source < N_ROW)).astype(jnp.float32)
            clipped = jnp.clip(source, 0, N_ROW - 1).astype(jnp.int32)
            window = lax.dynamic_index_in_dim(windows, clipped, 0, keepdims=False).astype(jnp.float32)
            strip_rows = window[:, :, place * MU_DEV:(place + 1) * MU_DEV]
            strip = jnp.einsum('pjm,pjn->mn', strip_rows, window) * weight_scale
            framed = jnp.pad(strip, ((0, 0), (MU_DEV, MU_DEV)))[:, place * MU_DEV:place * MU_DEV + 3 * MU_DEV]
            summed = summed + inside * framed
        return summed

    result = lax.map(owner_rows, jnp.arange(N_ROW, dtype=jnp.int32))
    return result.reshape(NBF, 3 * MU_DEV)
```

```python
import jax
import jax.numpy as jnp
from jax import lax
from jax.experimental import pallas as pl
from jax.experimental.pallas import tpu as pltpu
from jax.sharding import PartitionSpec as P

BS = 256
OB = 64
ROWS = 512
BF16 = jnp.bfloat16
F32 = jnp.float32
PARTS = (((0, 192), (384, 512)), ((0, 128), (320, 512)))
RESTS = ((192, 384), (128, 320))
OWN = (((0, 64), (256, 448)), ((64, 256), (448, 512)))
VMEM = pl.BlockSpec(memory_space=pltpu.VMEM)
SMEM = pl.BlockSpec(memory_space=pltpu.SMEM)


def pair_up(left, right):
    return jnp.concatenate([left[:, OB:], right[:, :OB]], axis=1)


def prep_kernel(orb_ref, own_ref, send_ref, buf, sems):
    d = lax.axis_index("row")
    core = lax.axis_index("aux") % 2
    odd = d % 2
    base = (d - 2 - odd) // 2
    last = orb_ref.shape[1] // 128 - 1
    copies = []
    for j in range(3):
        group = jnp.clip(base + j, 0, last)
        copies.append(
            pltpu.make_async_copy(
                orb_ref.at[:, pl.ds(pl.multiple_of(group * 128, 128), 128)],
                buf.at[j],
                sems.at[j],
            )
        )
    for copy in copies:
        copy.start()
    for copy in copies:
        copy.wait()
    b = [buf[j] for j in range(3)]
    line = [b[0], pair_up(b[0], b[1]), b[1], pair_up(b[1], b[2]), b[2]]
    pairs = [jnp.where(odd == 1, line[j + 1], line[j]) for j in range(4)]
    own_ref[:, :128] = pairs[1]
    own_ref[:, 128:] = pairs[2]
    send_ref[:, :128] = jnp.where(core == 0, pairs[2], pairs[0])
    send_ref[:, 128:] = jnp.where(core == 0, pairs[3], pairs[1])


def prep(orbitals):
    rows = orbitals.shape[0]
    return pl.pallas_call(
        prep_kernel,
        name="prep",
        out_shape=[jax.ShapeDtypeStruct((rows, 256), BF16)] * 2,
        in_specs=[pl.BlockSpec(memory_space=pl.ANY)],
        out_specs=[VMEM, VMEM],
        scratch_shapes=[pltpu.VMEM((3, rows, 128), BF16), pltpu.SemaphoreType.DMA((3,))],
    )(orbitals)


def half_kernel(
    cols_ref, mask_ref, int_ref, own_ref, got_ref, swp_ref,
    x_ref, xb_ref, q1_ref, q2_ref, q3_ref, q4_ref, rhs,
):
    p, r = pl.program_id(0), pl.program_id(1)
    d = lax.axis_index("row")
    core = lax.axis_index("aux") % 2

    @pl.when((p == 0) & (r == 0))
    def _():
        for c in range(2):
            first, second = (slice(0, 128), slice(128, 256))
            if c:
                first, second = second, first
            sources = (got_ref, own_ref, swp_ref) if c == 0 else (swp_ref, own_ref, got_ref)

            @pl.when(core == c)
            def _():
                for j, source in enumerate(sources):
                    for h in range(2):
                        rows = slice(h * BS, (h + 1) * BS)
                        rhs[2 * j + h, :, :128] = source[rows, first]
                        rhs[2 * j + h, :, 128:] = source[rows, second]

    acc = jnp.zeros((BS, 256), F32)
    for k in range(4):
        index = cols_ref[r, k] - 2 * (d - 1)
        acc = acc + jnp.dot(int_ref[0, 0, k], rhs[index], preferred_element_type=F32)
    count = mask_ref.shape[0]
    lane = lax.broadcasted_iota(jnp.int32, (1, 256), 1)
    factors = []
    for j in range(3):
        s = d - 1 + j
        inside = (s >= 0) & (s < count)
        value = mask_ref[jnp.clip(s, 0, count - 1), 2 * d + r]
        factors.append(jnp.where(inside, value, 0).astype(F32))
    low, mid, high = factors
    quarter = lane // OB
    f0 = jnp.where(core == 0, low, mid)
    f1 = jnp.where(core == 0, mid, high)
    f2 = jnp.where(core == 0, mid, low)
    f3 = jnp.where(core == 0, high, mid)
    factor = jnp.where(
        quarter == 0, f0, jnp.where(quarter == 1, f1, jnp.where(quarter == 2, f2, f3))
    )
    out = (acc * factor).astype(BF16)
    rows = pl.ds(pl.multiple_of(r * BS, BS), BS)
    lanes = pl.ds(pl.multiple_of(p * 128, 128), 128)
    x_ref[rows, lanes] = out[:, :128]
    xb_ref[rows, lanes] = out[:, 128:]

    @pl.when((p == pl.num_programs(0) - 1) & (r == pl.num_programs(1) - 1))
    def _():
        for c in range(2):

            @pl.when(core == c)
            def _():
                at = 0
                for start, end in PARTS[c]:
                    q1_ref[at : at + end - start] = xb_ref[start:end]
                    at += end - start
                at = 0
                for start, end in PARTS[1 - c]:
                    q3_ref[at : at + end - start] = x_ref[start:end]
                    at += end - start
                start, end = RESTS[1 - c]
                q2_ref[...] = x_ref[start:end]
                start, end = RESTS[c]
                q4_ref[...] = xb_ref[start:end]


def half_transform(block_columns, occ_mask, integrals, own, got, swapped):
    aux, rb, kept, bs, _ = integrals.shape
    whole = lambda p, r: (0, 0)
    lanes = aux * 128
    shapes = [(rb * bs, lanes)] * 2 + [(320, lanes), (192, lanes), (320, lanes), (192, lanes)]
    halo = pl.BlockSpec((rb * bs, 256), whole)
    return pl.pallas_call(
        half_kernel,
        name="half",
        out_shape=[jax.ShapeDtypeStruct(s, BF16) for s in shapes],
        grid=(aux, rb),
        in_specs=[
            SMEM,
            SMEM,
            pl.BlockSpec((1, 1, kept, bs, bs), lambda p, r: (p, r, 0, 0, 0)),
            halo,
            halo,
            halo,
        ],
        out_specs=[pl.BlockSpec(s, whole) for s in shapes],
        scratch_shapes=[pltpu.VMEM((3 * rb, bs, 256), BF16)],
    )(block_columns, occ_mask, integrals, own, got, swapped)


def nt(a, b):
    return lax.dot_general(a, b, (((1,), (1,)), ((), ())), preferred_element_type=F32)


def own_kernel(x_ref, xb_ref, xs_ref, xbs_ref, o_ref):
    core = lax.axis_index("aux") % 2
    lane = lax.broadcasted_iota(jnp.int32, (256, x_ref.shape[1]), 1)
    keep = ((lane // OB) % 2 == 1) == (core == 0)

    def picked(ref):
        both = [jnp.concatenate([ref[s:e] for s, e in OWN[c]], axis=0) for c in range(2)]
        return jnp.where(core == 0, both[0], both[1])

    total = None
    for ref, masked in ((x_ref, False), (xb_ref, True), (xs_ref, False), (xbs_ref, True)):
        rows = picked(ref)
        if masked:
            rows = jnp.where(keep, rows, jnp.zeros_like(rows))
        part = nt(rows, ref[...])
        total = part if total is None else total + part
    o_ref[...] = total


def own_part(x, xb, xs, xbs):
    return pl.pallas_call(
        own_kernel,
        name="own",
        out_shape=jax.ShapeDtypeStruct((256, x.shape[0]), F32),
        in_specs=[VMEM] * 4,
        out_specs=VMEM,
    )(x, xb, xs, xbs)


def off_kernel(
    x_ref, xb_ref, xs_ref, xbs_ref, q1_ref, q2_ref, q3_ref, q4_ref, o_ref,
    keep_ref, s1_ref, s2_ref, s3_ref, chunks,
):
    a = lax.axis_index("aux")
    core, y = a % 2, a // 2
    t = nt(q1_ref[...], x_ref[...]) + nt(q3_ref[...], xs_ref[...])
    u = nt(q2_ref[...], xb_ref[...]) + nt(q4_ref[...], xbs_ref[...])

    @pl.when(core == 0)
    def _():
        chunks[0] = t[:192]
        chunks[1, :128] = t[192:]
        chunks[1, 128:] = o_ref[:64]
        chunks[2] = o_ref[64:]
        chunks[3] = u

    @pl.when(core == 1)
    def _():
        chunks[0] = u
        chunks[1] = o_ref[:192]
        chunks[2, :64] = o_ref[192:]
        chunks[2, 64:] = t[:128]
        chunks[3] = t[128:]

    keep_ref[...] = chunks[y]
    for step, ref in enumerate((s1_ref, s2_ref, s3_ref)):
        ref[...] = chunks[(y + step + 1) % 4].astype(BF16)


def off_part(x, xb, xs, xbs, q1, q2, q3, q4, own):
    shape = (192, x.shape[0])
    return pl.pallas_call(
        off_kernel,
        name="off",
        out_shape=[jax.ShapeDtypeStruct(shape, F32)] + [jax.ShapeDtypeStruct(shape, BF16)] * 3,
        in_specs=[VMEM] * 9,
        out_specs=[VMEM] * 4,
        scratch_shapes=[pltpu.VMEM((4,) + shape, F32)],
    )(x, xb, xs, xbs, q1, q2, q3, q4, own)


def row_moves(rows, chips, core_0_up, cross):
    pairs = []
    for d in range(rows):
        for y in range(chips):
            for core in range(2):
                step = 1 if (core == 0) == core_0_up else -1
                if 0 <= d + step < rows:
                    target = 1 - core if cross else core
                    pairs.append(((2 * y + core) * rows + d, (2 * y + target) * rows + d + step))
    return pairs


def on_device(integrals, block_columns, orbitals, occ_mask):
    aux_devices, rows = lax.axis_size("aux"), lax.axis_size("row")
    chips = aux_devices // 2
    scale = 1.0 / (integrals.shape[0] * aux_devices * OB) ** 0.5

    def move(value, core_0_up, cross):
        return lax.ppermute(value, ("aux", "row"), row_moves(rows, chips, core_0_up, cross))

    def swap(value):
        return lax.ppermute(value, "aux", [(i, i ^ 1) for i in range(aux_devices)])

    def along_y(value, step):
        route = [(i, (i + 2 * step) % aux_devices) for i in range(aux_devices)]
        return lax.ppermute(value, "aux", route)

    own, send = prep(orbitals)
    got = move(send, True, False)
    swapped = swap(got)
    x, xb, q1, q2, q3, q4 = half_transform(
        block_columns, occ_mask.T, integrals, own, got, swapped
    )
    r1 = move(q1, True, False)
    r3 = move(q3, False, True)
    xs = swap(xb)
    xbs = swap(x)
    r2 = move(q2, False, False)
    r4 = move(q4, True, True)
    o = own_part(x, xb, xs, xbs)
    kept, s1, s2, s3 = off_part(x, xb, xs, xbs, r1, r2, r3, r4, o)
    total = kept
    for step, sent in enumerate((s1, s2, s3)):
        total = total + along_y(sent, step + 1).astype(F32)
    return (total * scale).T


def solution(mesh):
    in_specs = (P("aux", "row", None, None, None), P("row", None), P("row", None), P())
    out_specs = P("row", "aux")
    return jax.shard_map(
        on_device, mesh=mesh, in_specs=in_specs, out_specs=out_specs, check_vma=False
    )
```

```python
import jax
import jax.numpy as jnp
from jax import lax
from jax.experimental import pallas as pl
from jax.experimental.pallas import tpu as pltpu
from jax.sharding import PartitionSpec as P

BS = 256
OB = 64
BF16 = jnp.bfloat16
F32 = jnp.float32
PARTS = (((0, 192), (384, 512)), ((0, 128), (320, 512)))
RESTS = ((192, 384), (128, 320))
OWN = (((0, 64), (256, 448)), ((64, 256), (448, 512)))
VMEM = pl.BlockSpec(memory_space=pltpu.VMEM)
SMEM = pl.BlockSpec(memory_space=pltpu.SMEM)
ANY = pl.BlockSpec(memory_space=pl.ANY)


def on_chip(*values):
    return [pltpu.with_memory_space_constraint(v, pltpu.VMEM) for v in values]


def in_hbm(value):
    return pltpu.with_memory_space_constraint(value, pltpu.HBM)


def room(megabytes):
    return pltpu.CompilerParams(vmem_limit_bytes=megabytes * 2**20)


def cost(macs, sent):
    return pl.CostEstimate(flops=2 * macs, transcendentals=0, bytes_accessed=sent)


def pair_up(left, right):
    return jnp.concatenate([left[:, OB:], right[:, :OB]], axis=1)


def slice_pairs(orb_ref, buf, sems, others=()):
    d = lax.axis_index("row")
    odd = d % 2
    base = (d - 2 - odd) // 2
    last = orb_ref.shape[1] // 128 - 1
    copies = []
    for j in range(3):
        group = jnp.clip(base + j, 0, last)
        lanes = pl.ds(pl.multiple_of(group * 128, 128), 128)
        copies.append(pltpu.make_async_copy(orb_ref.at[:, lanes], buf.at[j], sems.at[j]))
    copies += others
    for copy in copies:
        copy.start()
    for copy in copies:
        copy.wait()
    b = [buf[j] for j in range(3)]
    line = [b[0], pair_up(b[0], b[1]), b[1], pair_up(b[1], b[2]), b[2]]
    return [jnp.where(odd == 1, line[j + 1], line[j]) for j in range(4)]


def send_kernel(orb_ref, send_ref, buf, sems):
    core = lax.axis_index("aux") % 2
    pairs = slice_pairs(orb_ref, buf, sems)
    send_ref[:, :128] = jnp.where(core == 0, pairs[2], pairs[0])
    send_ref[:, 128:] = jnp.where(core == 0, pairs[3], pairs[1])


def halo_to_send(orbitals):
    rows = orbitals.shape[0]
    return pl.pallas_call(
        send_kernel,
        name="send",
        cost_estimate=cost(512 * 1024, 2**20),
        compiler_params=room(4),
        out_shape=pltpu.VMEM((rows, 256), BF16),
        in_specs=[ANY],
        out_specs=VMEM,
        scratch_shapes=[pltpu.VMEM((3, rows, 128), BF16), pltpu.SemaphoreType.DMA((3,))],
    )(in_hbm(orbitals))


def stage_kernel(orb_ref, int_ref, own_ref, near_ref, buf, sems, int_sems):
    aux, rb = int_ref.shape[:2]
    loads = [
        pltpu.make_async_copy(int_ref.at[p, r], near_ref.at[p, r], int_sems.at[p, r])
        for p in range(aux)
        for r in range(rb)
    ]
    pairs = slice_pairs(orb_ref, buf, sems, loads)
    own_ref[:, :128] = pairs[1]
    own_ref[:, 128:] = pairs[2]


def stage(orbitals, integrals):
    rows = orbitals.shape[0]
    return pl.pallas_call(
        stage_kernel,
        name="stage",
        cost_estimate=cost(512 * 1024, 9 * 2**20),
        compiler_params=room(4),
        out_shape=[pltpu.VMEM((rows, 256), BF16), pltpu.VMEM(integrals.shape, BF16)],
        in_specs=[ANY, ANY],
        out_specs=[VMEM, VMEM],
        scratch_shapes=[
            pltpu.VMEM((3, rows, 128), BF16),
            pltpu.SemaphoreType.DMA((3,)),
            pltpu.SemaphoreType.DMA(integrals.shape[:2]),
        ],
    )(in_hbm(orbitals), in_hbm(integrals))


def half_kernel(
    cols_ref, mask_ref, int_ref, own_ref, got_ref, swp_ref,
    x_ref, xb_ref, q1_ref, q2_ref, q3_ref, q4_ref, rhs,
):
    d = lax.axis_index("row")
    core = lax.axis_index("aux") % 2
    aux, rb, kept = int_ref.shape[:3]

    for c in range(2):
        first, second = (slice(0, 128), slice(128, 256))
        if c:
            first, second = second, first
        sources = (got_ref, own_ref, swp_ref) if c == 0 else (swp_ref, own_ref, got_ref)

        @pl.when(core == c)
        def _():
            for j, source in enumerate(sources):
                for h in range(2):
                    rows = slice(h * BS, (h + 1) * BS)
                    rhs[2 * j + h, :, :128] = source[rows, first]
                    rhs[2 * j + h, :, 128:] = source[rows, second]

    count = mask_ref.shape[0]
    quarter = lax.broadcasted_iota(jnp.int32, (1, 256), 1) // OB
    for r in range(rb):
        factors = []
        for j in range(3):
            s = d - 1 + j
            inside = (s >= 0) & (s < count)
            value = mask_ref[jnp.clip(s, 0, count - 1), rb * d + r]
            factors.append(jnp.where(inside, value, 0).astype(F32))
        low, mid, high = factors
        f0 = jnp.where(core == 0, low, mid)
        f1 = jnp.where(core == 0, mid, high)
        f2 = jnp.where(core == 0, mid, low)
        f3 = jnp.where(core == 0, high, mid)
        factor = jnp.where(
            quarter == 0, f0, jnp.where(quarter == 1, f1, jnp.where(quarter == 2, f2, f3))
        )
        weights = jnp.concatenate([rhs[cols_ref[r, k] - rb * (d - 1)] for k in range(kept)], axis=0)
        for p in range(aux):
            left = jnp.concatenate([int_ref[p, r, k] for k in range(kept)], axis=1)
            acc = jnp.dot(left, weights, preferred_element_type=F32)
            out = (acc * factor).astype(BF16)
            x_ref[r * BS : (r + 1) * BS, p * 128 : (p + 1) * 128] = out[:, :128]
            xb_ref[r * BS : (r + 1) * BS, p * 128 : (p + 1) * 128] = out[:, 128:]

    for c in range(2):

        @pl.when(core == c)
        def _():
            at = 0
            for start, end in PARTS[c]:
                q1_ref[at : at + end - start] = xb_ref[start:end]
                at += end - start
            at = 0
            for start, end in PARTS[1 - c]:
                q3_ref[at : at + end - start] = x_ref[start:end]
                at += end - start
            start, end = RESTS[1 - c]
            q2_ref[...] = x_ref[start:end]
            start, end = RESTS[c]
            q4_ref[...] = xb_ref[start:end]


def half_transform(block_columns, occ_mask, integrals, own, got, swapped):
    aux, rb, kept, bs, _ = integrals.shape
    lanes = aux * 128
    shapes = [(rb * bs, lanes)] * 2 + [(320, lanes), (192, lanes), (320, lanes), (192, lanes)]
    return pl.pallas_call(
        half_kernel,
        name="half",
        cost_estimate=cost(512 * 1024 * 1024, 8 * 2**20),
        compiler_params=room(8),
        out_shape=[pltpu.VMEM(s, BF16) for s in shapes],
        in_specs=[SMEM, SMEM] + [VMEM] * 4,
        out_specs=[VMEM] * 6,
        scratch_shapes=[pltpu.VMEM((3 * rb, bs, 256), BF16)],
    )(block_columns, occ_mask, *on_chip(integrals, own, got, swapped))


def nt(a, b):
    return lax.dot_general(a, b, (((1,), (1,)), ((), ())), preferred_element_type=F32)


def own_kernel(x_ref, xb_ref, xs_ref, xbs_ref, o_ref):
    core = lax.axis_index("aux") % 2
    lane = lax.broadcasted_iota(jnp.int32, (256, x_ref.shape[1]), 1)
    keep = ((lane // OB) % 2 == 1) == (core == 0)

    def picked(ref):
        both = [jnp.concatenate([ref[s:e] for s, e in OWN[c]], axis=0) for c in range(2)]
        return jnp.where(core == 0, both[0], both[1])

    total = None
    for ref, masked in ((x_ref, False), (xb_ref, True), (xs_ref, False), (xbs_ref, True)):
        rows = picked(ref)
        if masked:
            rows = jnp.where(keep, rows, jnp.zeros_like(rows))
        part = nt(rows, ref[...])
        total = part if total is None else total + part
    o_ref[...] = total


def own_part(x, xb, xs, xbs):
    return pl.pallas_call(
        own_kernel,
        name="own",
        cost_estimate=cost(256 * 512 * 2048, 3 * 2**20),
        compiler_params=room(4),
        out_shape=pltpu.VMEM((256, x.shape[0]), F32),
        in_specs=[VMEM] * 4,
        out_specs=VMEM,
    )(*on_chip(x, xb, xs, xbs))


def off_kernel(
    x_ref, xb_ref, xs_ref, xbs_ref, q1_ref, q2_ref, q3_ref, q4_ref, o_ref,
    keep_ref, s1_ref, s2_ref, s3_ref, chunks,
):
    a = lax.axis_index("aux")
    core, y = a % 2, a // 2
    t = nt(q1_ref[...], x_ref[...]) + nt(q3_ref[...], xs_ref[...])
    u = nt(q2_ref[...], xb_ref[...]) + nt(q4_ref[...], xbs_ref[...])

    @pl.when(core == 0)
    def _():
        chunks[0] = t[:192]
        chunks[1, :128] = t[192:]
        chunks[1, 128:] = o_ref[:64]
        chunks[2] = o_ref[64:]
        chunks[3] = u

    @pl.when(core == 1)
    def _():
        chunks[0] = u
        chunks[1] = o_ref[:192]
        chunks[2, :64] = o_ref[192:]
        chunks[2, 64:] = t[:128]
        chunks[3] = t[128:]

    keep_ref[...] = chunks[y]
    for step, ref in enumerate((s1_ref, s2_ref, s3_ref)):
        ref[...] = chunks[(y + step + 1) % 4].astype(BF16)


def off_part(x, xb, xs, xbs, q1, q2, q3, q4, own):
    shape = (192, x.shape[0])
    return pl.pallas_call(
        off_kernel,
        name="off",
        cost_estimate=cost(512 * 512 * 1024, 6 * 2**20),
        compiler_params=room(8),
        out_shape=[pltpu.VMEM(shape, F32)] + [pltpu.VMEM(shape, BF16)] * 3,
        in_specs=[VMEM] * 9,
        out_specs=[VMEM] * 4,
        scratch_shapes=[pltpu.VMEM((4,) + shape, F32)],
    )(*on_chip(x, xb, xs, xbs, q1, q2, q3, q4, own))


def sum_kernel(scale, *refs):
    total = refs[0][...]
    for ref in refs[1:-1]:
        total = total + ref[...].astype(F32)
    refs[-1][...] = total * scale


def sum_parts(scale, parts):
    return pl.pallas_call(
        lambda *refs: sum_kernel(scale, *refs),
        name="sum",
        cost_estimate=cost(192 * 512, 2**20),
        compiler_params=room(4),
        out_shape=jax.ShapeDtypeStruct(parts[0].shape, F32),
        in_specs=[VMEM] * 4,
        out_specs=VMEM,
    )(*on_chip(*parts))


def row_moves(rows, chips, core_0_up, cross):
    pairs = []
    for d in range(rows):
        for y in range(chips):
            for core in range(2):
                step = 1 if (core == 0) == core_0_up else -1
                target = 1 - core if cross else core
                end = (2 * y + target) * rows + (d + step) % rows
                pairs.append(((2 * y + core) * rows + d, end))
    return pairs


def on_device(integrals, block_columns, orbitals, occ_mask):
    aux_devices, rows = lax.axis_size("aux"), lax.axis_size("row")
    chips = aux_devices // 2
    scale = 1.0 / (integrals.shape[0] * aux_devices * OB) ** 0.5

    def move(value, core_0_up, cross):
        return lax.ppermute(value, ("aux", "row"), row_moves(rows, chips, core_0_up, cross))

    def swap(value):
        return lax.ppermute(value, "aux", [(i, i ^ 1) for i in range(aux_devices)])

    def along_y(value, step):
        route = [(i, (i + 2 * step) % aux_devices) for i in range(aux_devices)]
        return lax.ppermute(value, "aux", route)

    send = halo_to_send(orbitals)
    got = move(send, True, False)
    own, near = stage(orbitals, integrals)
    got, own, near = lax.optimization_barrier((got, own, near))
    swapped = swap(got)
    x, xb, q1, q2, q3, q4 = half_transform(block_columns, occ_mask.T, near, own, got, swapped)
    r1 = move(q1, True, False)
    r3 = move(q3, False, True)
    xs = swap(xb)
    xbs = swap(x)
    r2 = move(q2, False, False)
    r4 = move(q4, True, True)
    o = own_part(x, xb, xs, xbs)
    kept, *sent = off_part(x, xb, xs, xbs, r1, r2, r3, r4, o)
    parts = [kept] + [along_y(value, step + 1) for step, value in enumerate(sent)]
    return sum_parts(scale, parts).T


def solution(mesh):
    in_specs = (P("aux", "row", None, None, None), P("row", None), P("row", None), P())
    out_specs = P("row", "aux")
    return jax.shard_map(
        on_device, mesh=mesh, in_specs=in_specs, out_specs=out_specs, check_vma=False
    )
```

```python
import functools

import jax
import jax.numpy as jnp
from jax import lax
from jax.experimental import pallas as pl
from jax.experimental.pallas import tpu as pltpu
from jax.sharding import PartitionSpec as P

BS = 256
OB = 64
BF16 = jnp.bfloat16
F32 = jnp.float32
PARTS = (((0, 192), (384, 512)), ((0, 128), (320, 512)))
RESTS = ((192, 384), (128, 320))
OWN = (((0, 64), (256, 448)), ((64, 256), (448, 512)))
VMEM = pl.BlockSpec(memory_space=pltpu.VMEM)
SMEM = pl.BlockSpec(memory_space=pltpu.SMEM)
ANY = pl.BlockSpec(memory_space=pl.ANY)


def on_chip(*values):
    return [pltpu.with_memory_space_constraint(v, pltpu.VMEM) for v in values]


def in_hbm(value):
    return pltpu.with_memory_space_constraint(value, pltpu.HBM)


def room(megabytes):
    return pltpu.CompilerParams(vmem_limit_bytes=megabytes * 2**20)


def cost(macs, sent):
    return pl.CostEstimate(flops=2 * macs, transcendentals=0, bytes_accessed=sent)


def pair_up(left, right):
    return jnp.concatenate([left[:, OB:], right[:, :OB]], axis=1)


def slice_pairs(orb_ref, buf, sems, others=()):
    d = lax.axis_index("row")
    odd = d % 2
    base = (d - 2 - odd) // 2
    last = orb_ref.shape[1] // 128 - 1
    copies = []
    for j in range(3):
        group = jnp.clip(base + j, 0, last)
        lanes = pl.ds(pl.multiple_of(group * 128, 128), 128)
        copies.append(pltpu.make_async_copy(orb_ref.at[:, lanes], buf.at[j], sems.at[j]))
    copies += others
    for copy in copies:
        copy.start()
    for copy in copies:
        copy.wait()
    b = [buf[j] for j in range(3)]
    line = [b[0], pair_up(b[0], b[1]), b[1], pair_up(b[1], b[2]), b[2]]
    return [jnp.where(odd == 1, line[j + 1], line[j]) for j in range(4)]


def send_kernel(orb_ref, send_ref, buf, sems):
    core = lax.axis_index("aux") % 2
    pairs = slice_pairs(orb_ref, buf, sems)
    send_ref[:, :128] = jnp.where(core == 0, pairs[2], pairs[0])
    send_ref[:, 128:] = jnp.where(core == 0, pairs[3], pairs[1])


def halo_to_send(orbitals):
    rows = orbitals.shape[0]
    return pl.pallas_call(
        send_kernel,
        name="send",
        cost_estimate=cost(512 * 1024, 2**20),
        compiler_params=room(4),
        out_shape=pltpu.VMEM((rows, 256), BF16),
        in_specs=[ANY],
        out_specs=VMEM,
        scratch_shapes=[pltpu.VMEM((3, rows, 128), BF16), pltpu.SemaphoreType.DMA((3,))],
    )(in_hbm(orbitals))


def stage_kernel(orb_ref, int_ref, own_ref, near_ref, buf, sems, int_sems):
    aux, rb = int_ref.shape[:2]
    loads = [
        pltpu.make_async_copy(int_ref.at[p, r], near_ref.at[p, r], int_sems.at[p, r])
        for p in range(aux)
        for r in range(rb)
    ]
    pairs = slice_pairs(orb_ref, buf, sems, loads)
    own_ref[:, :128] = pairs[1]
    own_ref[:, 128:] = pairs[2]


def stage(orbitals, integrals):
    rows = orbitals.shape[0]
    return pl.pallas_call(
        stage_kernel,
        name="stage",
        cost_estimate=cost(512 * 1024, 9 * 2**20),
        compiler_params=room(4),
        out_shape=[pltpu.VMEM((rows, 256), BF16), pltpu.VMEM(integrals.shape, BF16)],
        in_specs=[ANY, ANY],
        out_specs=[VMEM, VMEM],
        scratch_shapes=[
            pltpu.VMEM((3, rows, 128), BF16),
            pltpu.SemaphoreType.DMA((3,)),
            pltpu.SemaphoreType.DMA(integrals.shape[:2]),
        ],
    )(in_hbm(orbitals), in_hbm(integrals))


def half_kernel(
    cols_ref, mask_ref, int_ref, own_ref, got_ref, swp_ref,
    x_ref, xb_ref, q1_ref, q2_ref, q3_ref, q4_ref, rhs,
):
    d = lax.axis_index("row")
    core = lax.axis_index("aux") % 2
    aux, rb, kept = int_ref.shape[:3]

    for c in range(2):
        first, second = (slice(0, 128), slice(128, 256))
        if c:
            first, second = second, first
        sources = (got_ref, own_ref, swp_ref) if c == 0 else (swp_ref, own_ref, got_ref)

        @pl.when(core == c)
        def _():
            for j, source in enumerate(sources):
                for h in range(2):
                    rows = slice(h * BS, (h + 1) * BS)
                    rhs[2 * j + h, :, :128] = source[rows, first]
                    rhs[2 * j + h, :, 128:] = source[rows, second]

    count = mask_ref.shape[0]
    quarter = lax.broadcasted_iota(jnp.int32, (1, 256), 1) // OB
    for r in range(rb):
        factors = []
        for j in range(3):
            s = d - 1 + j
            inside = (s >= 0) & (s < count)
            value = mask_ref[jnp.clip(s, 0, count - 1), rb * d + r]
            factors.append(jnp.where(inside, value, 0).astype(F32))
        low, mid, high = factors
        f0 = jnp.where(core == 0, low, mid)
        f1 = jnp.where(core == 0, mid, high)
        f2 = jnp.where(core == 0, mid, low)
        f3 = jnp.where(core == 0, high, mid)
        factor = jnp.where(
            quarter == 0, f0, jnp.where(quarter == 1, f1, jnp.where(quarter == 2, f2, f3))
        )
        weights = jnp.concatenate([rhs[cols_ref[r, k] - rb * (d - 1)] for k in range(kept)], axis=0)
        for p in range(aux):
            left = jnp.concatenate([int_ref[p, r, k] for k in range(kept)], axis=1)
            acc = jnp.dot(left, weights, preferred_element_type=F32)
            out = (acc * factor).astype(BF16)
            x_ref[r * BS : (r + 1) * BS, p * 128 : (p + 1) * 128] = out[:, :128]
            xb_ref[r * BS : (r + 1) * BS, p * 128 : (p + 1) * 128] = out[:, 128:]

    for c in range(2):

        @pl.when(core == c)
        def _():
            at = 0
            for start, end in PARTS[c]:
                q1_ref[at : at + end - start] = xb_ref[start:end]
                at += end - start
            at = 0
            for start, end in PARTS[1 - c]:
                q3_ref[at : at + end - start] = x_ref[start:end]
                at += end - start
            start, end = RESTS[1 - c]
            q2_ref[...] = x_ref[start:end]
            start, end = RESTS[c]
            q4_ref[...] = xb_ref[start:end]


def half_transform(block_columns, occ_mask, integrals, own, got, swapped):
    aux, rb, kept, bs, _ = integrals.shape
    lanes = aux * 128
    shapes = [(rb * bs, lanes)] * 2 + [(320, lanes), (192, lanes), (320, lanes), (192, lanes)]
    return pl.pallas_call(
        half_kernel,
        name="half",
        cost_estimate=cost(512 * 1024 * 1024, 8 * 2**20),
        compiler_params=room(8),
        out_shape=[pltpu.VMEM(s, BF16) for s in shapes],
        in_specs=[SMEM, SMEM] + [VMEM] * 4,
        out_specs=[VMEM] * 6,
        scratch_shapes=[pltpu.VMEM((3 * rb, bs, 256), BF16)],
    )(block_columns, occ_mask, *on_chip(integrals, own, got, swapped))


def nt(a, b):
    return lax.dot_general(a, b, (((1,), (1,)), ((), ())), preferred_element_type=F32)


def own_kernel(x_ref, xb_ref, xs_ref, xbs_ref, o_ref):
    core = lax.axis_index("aux") % 2
    lane = lax.broadcasted_iota(jnp.int32, (256, x_ref.shape[1]), 1)
    keep = ((lane // OB) % 2 == 1) == (core == 0)

    def picked(ref):
        both = [jnp.concatenate([ref[s:e] for s, e in OWN[c]], axis=0) for c in range(2)]
        return jnp.where(core == 0, both[0], both[1])

    total = None
    for ref, masked in ((x_ref, False), (xb_ref, True), (xs_ref, False), (xbs_ref, True)):
        rows = picked(ref)
        if masked:
            rows = jnp.where(keep, rows, jnp.zeros_like(rows))
        part = nt(rows, ref[...])
        total = part if total is None else total + part
    o_ref[...] = total


def own_part(x, xb, xs, xbs):
    return pl.pallas_call(
        own_kernel,
        name="own",
        cost_estimate=cost(256 * 512 * 2048, 3 * 2**20),
        compiler_params=room(4),
        out_shape=pltpu.VMEM((256, x.shape[0]), F32),
        in_specs=[VMEM] * 4,
        out_specs=VMEM,
    )(*on_chip(x, xb, xs, xbs))


def off_kernel(
    last, x_ref, xb_ref, xs_ref, xbs_ref, q1_ref, q2_ref, q3_ref, q4_ref, o_ref,
    keep_ref, s1_ref, s2_ref, s3_ref, chunks,
):
    a = lax.axis_index("aux")
    core, y = a % 2, a // 2
    d = lax.axis_index("row")
    t = nt(q1_ref[...], x_ref[...]) + nt(q3_ref[...], xs_ref[...])
    u = nt(q2_ref[...], xb_ref[...]) + nt(q4_ref[...], xbs_ref[...])
    t = jnp.where(d == jnp.where(core == 0, 0, last), 0.0, t)
    u = jnp.where(d == jnp.where(core == 0, last, 0), 0.0, u)

    @pl.when(core == 0)
    def _():
        chunks[0] = t[:192]
        chunks[1, :128] = t[192:]
        chunks[1, 128:] = o_ref[:64]
        chunks[2] = o_ref[64:]
        chunks[3] = u

    @pl.when(core == 1)
    def _():
        chunks[0] = u
        chunks[1] = o_ref[:192]
        chunks[2, :64] = o_ref[192:]
        chunks[2, 64:] = t[:128]
        chunks[3] = t[128:]

    keep_ref[...] = chunks[y]
    for step, ref in enumerate((s1_ref, s2_ref, s3_ref)):
        ref[...] = chunks[(y + step + 1) % 4].astype(BF16)


def off_part(last, x, xb, xs, xbs, q1, q2, q3, q4, own):
    shape = (192, x.shape[0])
    return pl.pallas_call(
        functools.partial(off_kernel, last),
        name="off",
        cost_estimate=cost(512 * 512 * 1024, 6 * 2**20),
        compiler_params=room(8),
        out_shape=[pltpu.VMEM(shape, F32)] + [pltpu.VMEM(shape, BF16)] * 3,
        in_specs=[VMEM] * 9,
        out_specs=[VMEM] * 4,
        scratch_shapes=[pltpu.VMEM((4,) + shape, F32)],
    )(*on_chip(x, xb, xs, xbs, q1, q2, q3, q4, own))


def sum_kernel(scale, *refs):
    total = refs[0][...]
    for ref in refs[1:-1]:
        total = total + ref[...].astype(F32)
    refs[-1][...] = total * scale


def sum_parts(scale, parts):
    return pl.pallas_call(
        lambda *refs: sum_kernel(scale, *refs),
        name="sum",
        cost_estimate=cost(192 * 512, 2**20),
        compiler_params=room(4),
        out_shape=jax.ShapeDtypeStruct(parts[0].shape, F32),
        in_specs=[VMEM] * 4,
        out_specs=VMEM,
    )(*on_chip(*parts))


def row_moves(rows, chips, core_0_up, cross):
    pairs = []
    for d in range(rows):
        for y in range(chips):
            for core in range(2):
                step = 1 if (core == 0) == core_0_up else -1
                inside = 0 <= d + step < rows
                target = 1 - core if cross == inside else core
                end = d + step if inside else d
                chip = (y + 1) % chips if cross and not inside else y
                pairs.append(((2 * y + core) * rows + d, (2 * chip + target) * rows + end))
    return pairs


def on_device(integrals, block_columns, orbitals, occ_mask):
    aux_devices, rows = lax.axis_size("aux"), lax.axis_size("row")
    chips = aux_devices // 2
    scale = 1.0 / (integrals.shape[0] * aux_devices * OB) ** 0.5

    def move(value, core_0_up, cross):
        return lax.ppermute(value, ("aux", "row"), row_moves(rows, chips, core_0_up, cross))

    def swap(value):
        return lax.ppermute(value, "aux", [(i, i ^ 1) for i in range(aux_devices)])

    def along_y(value, step):
        route = [(i, (i + 2 * step) % aux_devices) for i in range(aux_devices)]
        return lax.ppermute(value, "aux", route)

    send = halo_to_send(orbitals)
    got = move(send, True, False)
    own, near = stage(orbitals, integrals)
    got, own, near = lax.optimization_barrier((got, own, near))
    swapped = swap(got)
    x, xb, q1, q2, q3, q4 = half_transform(block_columns, occ_mask.T, near, own, got, swapped)
    r1 = move(q1, True, False)
    r3 = move(q3, False, True)
    xs = swap(xb)
    xbs = swap(x)
    r2 = move(q2, False, False)
    r4 = move(q4, True, True)
    o = own_part(x, xb, xs, xbs)
    kept, *sent = off_part(rows - 1, x, xb, xs, xbs, r1, r2, r3, r4, o)
    parts = [kept] + [along_y(sent[step - 1], step) for step in (2, 1, 3)]
    return sum_parts(scale, parts).T


def solution(mesh):
    in_specs = (P("aux", "row", None, None, None), P("row", None), P("row", None), P())
    out_specs = P("row", "aux")
    return jax.shard_map(
        on_device, mesh=mesh, in_specs=in_specs, out_specs=out_specs, check_vma=False
    )
```

```python
import functools

import jax
import jax.numpy as jnp
from jax import lax
from jax.experimental import pallas as pl
from jax.experimental.pallas import tpu as pltpu
from jax.sharding import PartitionSpec as P

BS = 256
OB = 64
GROUP = 2
BF16 = jnp.bfloat16
F32 = jnp.float32
PARTS = (((0, 192), (384, 512)), ((0, 128), (320, 512)))
RESTS = ((192, 384), (128, 320))
OWN = (((0, 64), (256, 448)), ((64, 256), (448, 512)))
VMEM = pl.BlockSpec(memory_space=pltpu.VMEM)
SMEM = pl.BlockSpec(memory_space=pltpu.SMEM)
ANY = pl.BlockSpec(memory_space=pl.ANY)


def on_chip(*values):
    return [pltpu.with_memory_space_constraint(v, pltpu.VMEM) for v in values]


def in_hbm(value):
    return pltpu.with_memory_space_constraint(value, pltpu.HBM)


def room(megabytes):
    return pltpu.CompilerParams(vmem_limit_bytes=megabytes * 2**20)


def cost(macs, sent):
    return pl.CostEstimate(flops=2 * macs, transcendentals=0, bytes_accessed=sent)


def pair_up(left, right):
    return jnp.concatenate([left[:, OB:], right[:, :OB]], axis=1)


def load_groups(orb_ref, first, buf, sems):
    last = orb_ref.shape[1] // 128 - 1
    copies = []
    for j in range(buf.shape[0]):
        group = jnp.clip(first + j, 0, last)
        lanes = pl.ds(pl.multiple_of(group * 128, 128), 128)
        copies.append(pltpu.make_async_copy(orb_ref.at[:, lanes], buf.at[j], sems.at[j]))
    return copies


def send_kernel(orb_ref, send_ref, buf, sems):
    d = lax.axis_index("row")
    core = lax.axis_index("aux") % 2
    odd = d % 2
    copies = load_groups(orb_ref, (d - 2 - odd) // 2 + 1 - core, buf, sems)
    for copy in copies:
        copy.start()
    for copy in copies:
        copy.wait()
    rows = buf.shape[1]
    half = rows // 2

    @pl.when(odd == 0)
    def _():
        send_ref[:rows] = buf[0]
        send_ref[rows:] = jnp.concatenate([buf[1, :half, :OB], buf[1, half:, :OB]], axis=1)

    @pl.when(odd == 1)
    def _():
        send_ref[:rows] = pair_up(buf[0], buf[1])
        send_ref[rows:] = jnp.concatenate([buf[1, :half, OB:], buf[1, half:, OB:]], axis=1)


def halo_to_send(orbitals):
    rows = orbitals.shape[0]
    return pl.pallas_call(
        send_kernel,
        name="send",
        cost_estimate=cost(512 * 1024, 2**20),
        compiler_params=room(4),
        out_shape=pltpu.VMEM((rows + rows // 2, 128), BF16),
        in_specs=[ANY],
        out_specs=VMEM,
        scratch_shapes=[pltpu.VMEM((2, rows, 128), BF16), pltpu.SemaphoreType.DMA((2,))],
    )(in_hbm(orbitals))


def stage_kernel(
    cols_hbm, mask_hbm, orb_ref, int_ref, own_ref, near_ref, factor_ref, local_ref,
    cols_ref, mask_ref, buf, sems, int_sems, table_sems,
):
    aux, rb, kept = int_ref.shape[:3]
    loads = [
        pltpu.make_async_copy(int_ref.at[p, r], near_ref.at[p, r], int_sems.at[p, r])
        for p in range(aux)
        for r in range(rb)
    ]
    d = lax.axis_index("row")
    odd = d % 2
    copies = load_groups(orb_ref, (d - 2 - odd) // 2, buf, sems) + loads
    tables = [
        pltpu.make_async_copy(cols_hbm, cols_ref, table_sems.at[0]),
        pltpu.make_async_copy(mask_hbm, mask_ref, table_sems.at[1]),
    ]
    for copy in tables + copies:
        copy.start()
    for copy in tables:
        copy.wait()
    core = lax.axis_index("aux") % 2
    count = mask_ref.shape[0]
    quarter = lax.broadcasted_iota(jnp.int32, (1, 256), 1) // OB
    for r in range(rb):
        factors = []
        for j in range(3):
            s = d - 1 + j
            inside = (s >= 0) & (s < count)
            value = mask_ref[jnp.clip(s, 0, count - 1), rb * d + r]
            factors.append(jnp.where(inside, value, 0).astype(F32))
        low, mid, high = factors
        f0 = jnp.where(core == 0, low, mid)
        f1 = jnp.where(core == 0, mid, high)
        f2 = jnp.where(core == 0, mid, low)
        f3 = jnp.where(core == 0, high, mid)
        factor = jnp.where(
            quarter == 0, f0, jnp.where(quarter == 1, f1, jnp.where(quarter == 2, f2, f3))
        )
        factor_ref[r : r + 1] = factor
        for k in range(kept):
            local_ref[r, k] = cols_ref[r, k] - rb * (d - 1)
    for copy in copies:
        copy.wait()

    @pl.when(odd == 0)
    def _():
        own_ref[:, :128] = pair_up(buf[0], buf[1])
        own_ref[:, 128:] = buf[1]

    @pl.when(odd == 1)
    def _():
        own_ref[:, :128] = buf[1]
        own_ref[:, 128:] = pair_up(buf[1], buf[2])


def stage(block_columns, occ_mask, orbitals, integrals):
    rows, rb = orbitals.shape[0], integrals.shape[1]
    return pl.pallas_call(
        stage_kernel,
        name="stage",
        cost_estimate=cost(512 * 1024, 9 * 2**20),
        compiler_params=room(4),
        out_shape=[
            pltpu.VMEM((rows, 256), BF16),
            pltpu.VMEM(integrals.shape, BF16),
            pltpu.VMEM((rb, 256), F32),
            pltpu.SMEM(block_columns.shape, jnp.int32),
        ],
        in_specs=[ANY] * 4,
        out_specs=[VMEM, VMEM, VMEM, SMEM],
        scratch_shapes=[
            pltpu.SMEM(block_columns.shape, jnp.int32),
            pltpu.SMEM(occ_mask.shape, jnp.int32),
            pltpu.VMEM((3, rows, 128), BF16),
            pltpu.SemaphoreType.DMA((3,)),
            pltpu.SemaphoreType.DMA(integrals.shape[:2]),
            pltpu.SemaphoreType.DMA((2,)),
        ],
    )(*[in_hbm(v) for v in (block_columns, occ_mask, orbitals, integrals)])


def half_kernel(
    cols_ref, factor_ref, int_ref, own_ref, got_ref, swp_ref,
    x_ref, q1_ref, q2_ref, q3_ref, q4_ref, rhs,
):
    core = lax.axis_index("aux") % 2
    aux, rb, kept = int_ref.shape[:3]

    for c in range(2):
        first, second = (slice(0, 128), slice(128, 256))
        if c:
            first, second = second, first

        @pl.when(core == c)
        def _():
            for h in range(rb):
                rows = slice(h * BS, (h + 1) * BS)
                rhs[rb + h, :, :128] = own_ref[rows, first]
                rhs[rb + h, :, 128:] = own_ref[rows, second]
            for j, source in ((0, got_ref if c == 0 else swp_ref), (2, swp_ref if c == 0 else got_ref)):
                for h in range(rb):
                    pair = source[h * BS : (h + 1) * BS]
                    third = source[rb * BS :, h * OB : (h + 1) * OB]
                    rhs[rb * j + h, :, first] = pair
                    rhs[rb * j + h, :, second] = jnp.concatenate([pair[:, OB:], third], axis=1)

    for r in range(rb):
        factor = factor_ref[r : r + 1]
        weights = jnp.concatenate([rhs[cols_ref[r, k]] for k in range(kept)], axis=0)
        for start in range(0, aux, GROUP):
            left = jnp.concatenate(
                [int_ref[start : start + GROUP, r, k].reshape(GROUP * BS, BS) for k in range(kept)], axis=1
            )
            acc = jnp.dot(left, weights, preferred_element_type=F32)
            out = (acc * factor).astype(BF16)
            for j in range(GROUP):
                lanes = slice((start + j) * 128, (start + j + 1) * 128)
                x_ref[0, r * BS : (r + 1) * BS, lanes] = out[j * BS : (j + 1) * BS, :128]
                x_ref[1, r * BS : (r + 1) * BS, lanes] = out[j * BS : (j + 1) * BS, 128:]

    for c in range(2):

        @pl.when(core == c)
        def _():
            at = 0
            for start, end in PARTS[c]:
                q1_ref[at : at + end - start] = x_ref[1, start:end]
                at += end - start
            at = 0
            for start, end in PARTS[1 - c]:
                q3_ref[at : at + end - start] = x_ref[0, start:end]
                at += end - start
            start, end = RESTS[1 - c]
            q2_ref[...] = x_ref[0, start:end]
            start, end = RESTS[c]
            q4_ref[...] = x_ref[1, start:end]


def half_transform(columns, factors, integrals, own, got, swapped):
    aux, rb, kept, bs, _ = integrals.shape
    lanes = aux * 128
    shapes = [(2, rb * bs, lanes)] + [(320, lanes), (192, lanes), (320, lanes), (192, lanes)]
    return pl.pallas_call(
        half_kernel,
        name="half",
        cost_estimate=cost(512 * 1024 * 1024, 8 * 2**20),
        compiler_params=room(8),
        out_shape=[pltpu.VMEM(s, BF16) for s in shapes],
        in_specs=[SMEM] + [VMEM] * 5,
        out_specs=[VMEM] * 5,
        scratch_shapes=[pltpu.VMEM((3 * rb, bs, 256), BF16)],
    )(pltpu.with_memory_space_constraint(columns, pltpu.SMEM), *on_chip(factors, integrals, own, got, swapped))


def nt(a, b):
    return lax.dot_general(a, b, (((1,), (1,)), ((), ())), preferred_element_type=F32)


def own_kernel(x_ref, s_ref, o_ref):
    core = lax.axis_index("aux") % 2
    lane = lax.broadcasted_iota(jnp.int32, (256, x_ref.shape[2]), 1)
    keep = ((lane // OB) % 2 == 1) == (core == 0)

    def picked(ref):
        both = [jnp.concatenate([ref[s:e] for s, e in OWN[c]], axis=0) for c in range(2)]
        return jnp.where(core == 0, both[0], both[1])

    total = None
    for ref, masked in (
        (x_ref.at[0], False), (x_ref.at[1], True), (s_ref.at[1], False), (s_ref.at[0], True),
    ):
        rows = picked(ref)
        if masked:
            rows = jnp.where(keep, rows, jnp.zeros_like(rows))
        part = nt(rows, ref[...])
        total = part if total is None else total + part
    o_ref[...] = total


def own_part(x, s):
    return pl.pallas_call(
        own_kernel,
        name="own",
        cost_estimate=cost(256 * 512 * 2048, 3 * 2**20),
        compiler_params=room(4),
        out_shape=pltpu.VMEM((256, x.shape[1]), F32),
        in_specs=[VMEM] * 2,
        out_specs=VMEM,
    )(*on_chip(x, s))


def near_kernel(last, x_ref, s_ref, q1_ref, q3_ref, t_ref):
    d, core = lax.axis_index("row"), lax.axis_index("aux") % 2
    t = nt(q1_ref[...], x_ref[0]) + nt(q3_ref[...], s_ref[1])
    t_ref[...] = jnp.where(d == jnp.where(core == 0, 0, last), 0.0, t)


def near_part(last, x, s, q1, q3):
    return pl.pallas_call(
        functools.partial(near_kernel, last),
        name="near",
        cost_estimate=cost(320 * 512 * 1024, 2 * 2**20),
        compiler_params=room(4),
        out_shape=pltpu.VMEM((320, x.shape[1]), F32),
        in_specs=[VMEM] * 4,
        out_specs=VMEM,
    )(*on_chip(x, s, q1, q3))


def off_kernel(
    last, x_ref, s_ref, q2_ref, q4_ref, o_ref, t_ref, keep_ref, s1_ref, s2_ref, s3_ref, chunks,
):
    a = lax.axis_index("aux")
    core, y = a % 2, a // 2
    d = lax.axis_index("row")
    u = nt(q2_ref[...], x_ref[1]) + nt(q4_ref[...], s_ref[0])
    u = jnp.where(d == jnp.where(core == 0, last, 0), 0.0, u)

    @pl.when(core == 0)
    def _():
        chunks[0] = t_ref[:192]
        chunks[1, :128] = t_ref[192:]
        chunks[1, 128:] = o_ref[:64]
        chunks[2] = o_ref[64:]
        chunks[3] = u

    @pl.when(core == 1)
    def _():
        chunks[0] = u
        chunks[1] = o_ref[:192]
        chunks[2, :64] = o_ref[192:]
        chunks[2, 64:] = t_ref[:128]
        chunks[3] = t_ref[128:]

    keep_ref[...] = chunks[y]
    for step, ref in enumerate((s1_ref, s2_ref, s3_ref)):
        ref[...] = chunks[(y + step + 1) % 4].astype(BF16)


def off_part(last, x, s, q2, q4, own, near):
    shape = (192, x.shape[1])
    return pl.pallas_call(
        functools.partial(off_kernel, last),
        name="off",
        cost_estimate=cost(192 * 512 * 1024, 4 * 2**20),
        compiler_params=room(8),
        out_shape=[pltpu.VMEM(shape, F32)] + [pltpu.VMEM(shape, BF16)] * 3,
        in_specs=[VMEM] * 6,
        out_specs=[VMEM] * 4,
        scratch_shapes=[pltpu.VMEM((4,) + shape, F32)],
    )(*on_chip(x, s, q2, q4, own, near))


def sum_kernel(scale, *refs):
    rows = refs[-1].shape[0]
    at = pl.ds(pl.multiple_of(pl.program_id(0) * rows, rows), rows)
    total = refs[0][at]
    for ref in refs[1:-1]:
        total = total + ref[at].astype(F32)
    refs[-1][...] = total * scale


def sum_parts(scale, parts):
    rows, columns = parts[0].shape
    steps = 1
    return pl.pallas_call(
        functools.partial(sum_kernel, scale),
        name="sum",
        cost_estimate=cost(192 * 512, 2**20),
        compiler_params=room(4),
        grid=(steps,),
        out_shape=jax.ShapeDtypeStruct((rows, columns), F32),
        in_specs=[VMEM] * 4,
        out_specs=pl.BlockSpec((rows // steps, columns), lambda i: (i, 0)),
    )(*on_chip(*parts))


def row_moves(rows, chips, core_0_up, cross):
    pairs = []
    for d in range(rows):
        for y in range(chips):
            for core in range(2):
                step = 1 if (core == 0) == core_0_up else -1
                inside = 0 <= d + step < rows
                target = 1 - core if cross == inside else core
                end = d + step if inside else d
                chip = (y + 1) % chips if cross and not inside else y
                pairs.append(((2 * y + core) * rows + d, (2 * chip + target) * rows + end))
    return pairs


def on_device(integrals, block_columns, orbitals, occ_mask):
    aux_devices, rows = lax.axis_size("aux"), lax.axis_size("row")
    chips = aux_devices // 2
    scale = 1.0 / (integrals.shape[0] * aux_devices * OB) ** 0.5

    def move(value, core_0_up, cross):
        return lax.ppermute(value, ("aux", "row"), row_moves(rows, chips, core_0_up, cross))

    def swap(value):
        return lax.ppermute(value, "aux", [(i, i ^ 1) for i in range(aux_devices)])

    def along_y(value, step):
        route = [(i, (i + 2 * step) % aux_devices) for i in range(aux_devices)]
        return lax.ppermute(value, "aux", route)

    send = halo_to_send(orbitals)
    got = move(send, True, False)
    own, near, factors, columns = stage(block_columns, occ_mask.T, orbitals, integrals)
    got, own, near, factors, columns = lax.optimization_barrier((got, own, near, factors, columns))
    swapped = swap(got)
    x, q1, q2, q3, q4 = half_transform(columns, factors, near, own, got, swapped)
    r1 = move(q1, True, False)
    r3 = move(q3, False, True)
    others = swap(x)
    r2 = move(q2, False, False)
    r4 = move(q4, True, True)
    o = own_part(x, others)
    t = near_part(rows - 1, x, others, r1, r3)
    kept, *sent = off_part(rows - 1, x, others, r2, r4, o, t)
    parts = [kept] + [along_y(sent[step - 1], step) for step in (2, 1, 3)]
    return sum_parts(scale, parts).T


def solution(mesh):
    in_specs = (P("aux", "row", None, None, None), P("row", None), P("row", None), P())
    out_specs = P("row", "aux")
    return jax.shard_map(
        on_device, mesh=mesh, in_specs=in_specs, out_specs=out_specs, check_vma=False
    )
```

```python
import functools

import jax
import jax.numpy as jnp
from jax import lax
from jax.experimental import pallas as pl
from jax.experimental.pallas import tpu as pltpu
from jax.sharding import PartitionSpec as P

BS = 256
OB = 64
SPLIT = 4
GROUP = 2
BF16 = jnp.bfloat16
F32 = jnp.float32
PARTS = (((0, 192), (384, 512)), ((0, 128), (320, 512)))
RESTS = ((192, 384), (128, 320))
OWN = (((0, 64), (256, 448)), ((64, 256), (448, 512)))
VMEM = pl.BlockSpec(memory_space=pltpu.VMEM)
SMEM = pl.BlockSpec(memory_space=pltpu.SMEM)
ANY = pl.BlockSpec(memory_space=pl.ANY)


def on_chip(*values):
    return [pltpu.with_memory_space_constraint(v, pltpu.VMEM) for v in values]


def in_hbm(value):
    return pltpu.with_memory_space_constraint(value, pltpu.HBM)


def room(megabytes):
    return pltpu.CompilerParams(vmem_limit_bytes=megabytes * 2**20)


def cost(macs, sent):
    return pl.CostEstimate(flops=2 * macs, transcendentals=0, bytes_accessed=sent)


def pair_up(left, right):
    return jnp.concatenate([left[:, OB:], right[:, :OB]], axis=1)


def load_groups(orb_ref, first, buf, sems, parts=1):
    last = orb_ref.shape[1] // 128 - 1
    copies = []
    for j in range(buf.shape[0]):
        group = jnp.clip(first + j, 0, last)
        lanes = pl.ds(pl.multiple_of(group * 128, 128), 128)
        for part in range(parts):
            rows = pl.ds(part * (buf.shape[1] // parts), buf.shape[1] // parts)
            copies.append(
                pltpu.make_async_copy(
                    orb_ref.at[rows, lanes], buf.at[j, rows], sems.at[j * parts + part]
                )
            )
    return copies


def send_kernel(orb_ref, send_ref, buf, sems):
    d = lax.axis_index("row")
    core = lax.axis_index("aux") % 2
    odd = d % 2
    copies = load_groups(orb_ref, (d - 2 - odd) // 2 + 1 - core, buf, sems, SPLIT)
    for copy in copies:
        copy.start()
    for copy in copies:
        copy.wait()
    rows = buf.shape[1]
    half = rows // 2

    @pl.when(odd == 0)
    def _():
        send_ref[:rows] = buf[0]
        send_ref[rows:] = jnp.concatenate([buf[1, :half, :OB], buf[1, half:, :OB]], axis=1)

    @pl.when(odd == 1)
    def _():
        send_ref[:rows] = pair_up(buf[0], buf[1])
        send_ref[rows:] = jnp.concatenate([buf[1, :half, OB:], buf[1, half:, OB:]], axis=1)


def halo_to_send(orbitals):
    rows = orbitals.shape[0]
    return pl.pallas_call(
        send_kernel,
        name="send",
        cost_estimate=cost(512 * 1024, 2**20),
        compiler_params=room(4),
        out_shape=pltpu.VMEM((rows + rows // 2, 128), BF16),
        in_specs=[ANY],
        out_specs=VMEM,
        scratch_shapes=[pltpu.VMEM((2, rows, 128), BF16), pltpu.SemaphoreType.DMA((2 * SPLIT,))],
    )(in_hbm(orbitals))


def stage_kernel(
    cols_hbm, mask_hbm, orb_ref, int_ref, own_ref, near_ref, factor_ref, local_ref,
    cols_ref, mask_ref, buf, sems, int_sems, table_sems,
):
    aux, rb, kept = int_ref.shape[:3]
    loads = [
        pltpu.make_async_copy(int_ref.at[p, r], near_ref.at[p, r], int_sems.at[p, r])
        for p in range(aux)
        for r in range(rb)
    ]
    d = lax.axis_index("row")
    odd = d % 2
    copies = load_groups(orb_ref, (d - 2 - odd) // 2, buf, sems) + loads
    tables = [
        pltpu.make_async_copy(cols_hbm, cols_ref, table_sems.at[0]),
        pltpu.make_async_copy(mask_hbm, mask_ref, table_sems.at[1]),
    ]
    for copy in tables + copies:
        copy.start()
    for copy in tables:
        copy.wait()
    core = lax.axis_index("aux") % 2
    count = mask_ref.shape[0]
    quarter = lax.broadcasted_iota(jnp.int32, (1, 256), 1) // OB
    for r in range(rb):
        factors = []
        for j in range(3):
            s = d - 1 + j
            inside = (s >= 0) & (s < count)
            value = mask_ref[jnp.clip(s, 0, count - 1), rb * d + r]
            factors.append(jnp.where(inside, value, 0).astype(F32))
        low, mid, high = factors
        f0 = jnp.where(core == 0, low, mid)
        f1 = jnp.where(core == 0, mid, high)
        f2 = jnp.where(core == 0, mid, low)
        f3 = jnp.where(core == 0, high, mid)
        factor = jnp.where(
            quarter == 0, f0, jnp.where(quarter == 1, f1, jnp.where(quarter == 2, f2, f3))
        )
        factor_ref[r : r + 1] = factor
        for k in range(kept):
            local_ref[r, k] = cols_ref[r, k] - rb * (d - 1)
    for copy in copies:
        copy.wait()

    @pl.when(odd == 0)
    def _():
        own_ref[:, :128] = pair_up(buf[0], buf[1])
        own_ref[:, 128:] = buf[1]

    @pl.when(odd == 1)
    def _():
        own_ref[:, :128] = buf[1]
        own_ref[:, 128:] = pair_up(buf[1], buf[2])


def stage(block_columns, occ_mask, orbitals, integrals):
    rows, rb = orbitals.shape[0], integrals.shape[1]
    return pl.pallas_call(
        stage_kernel,
        name="stage",
        cost_estimate=cost(512 * 1024, 9 * 2**20),
        compiler_params=room(4),
        out_shape=[
            pltpu.VMEM((rows, 256), BF16),
            pltpu.VMEM(integrals.shape, BF16),
            pltpu.VMEM((rb, 256), F32),
            pltpu.SMEM(block_columns.shape, jnp.int32),
        ],
        in_specs=[ANY] * 4,
        out_specs=[VMEM, VMEM, VMEM, SMEM],
        scratch_shapes=[
            pltpu.SMEM(block_columns.shape, jnp.int32),
            pltpu.SMEM(occ_mask.shape, jnp.int32),
            pltpu.VMEM((3, rows, 128), BF16),
            pltpu.SemaphoreType.DMA((3,)),
            pltpu.SemaphoreType.DMA(integrals.shape[:2]),
            pltpu.SemaphoreType.DMA((2,)),
        ],
    )(*[in_hbm(v) for v in (block_columns, occ_mask, orbitals, integrals)])


def half_kernel(
    cols_ref, factor_ref, int_ref, own_ref, got_ref, swp_ref,
    x_ref, q1_ref, q2_ref, q3_ref, q4_ref, rhs,
):
    core = lax.axis_index("aux") % 2
    aux, rb, kept = int_ref.shape[:3]

    for c in range(2):
        first, second = (slice(0, 128), slice(128, 256))
        if c:
            first, second = second, first

        @pl.when(core == c)
        def _():
            for h in range(rb):
                rows = slice(h * BS, (h + 1) * BS)
                rhs[rb + h, :, :128] = own_ref[rows, first]
                rhs[rb + h, :, 128:] = own_ref[rows, second]
            for j, source in ((0, got_ref if c == 0 else swp_ref), (2, swp_ref if c == 0 else got_ref)):
                for h in range(rb):
                    pair = source[h * BS : (h + 1) * BS]
                    third = source[rb * BS :, h * OB : (h + 1) * OB]
                    rhs[rb * j + h, :, first] = pair
                    rhs[rb * j + h, :, second] = jnp.concatenate([pair[:, OB:], third], axis=1)

    for r in range(rb):
        factor = factor_ref[r : r + 1]
        weights = jnp.concatenate([rhs[cols_ref[r, k]] for k in range(kept)], axis=0)
        for start in range(0, aux, GROUP):
            left = jnp.concatenate(
                [int_ref[start : start + GROUP, r, k].reshape(GROUP * BS, BS) for k in range(kept)], axis=1
            )
            acc = jnp.dot(left, weights, preferred_element_type=F32)
            out = (acc * factor).astype(BF16)
            for j in range(GROUP):
                lanes = slice((start + j) * 128, (start + j + 1) * 128)
                x_ref[0, r * BS : (r + 1) * BS, lanes] = out[j * BS : (j + 1) * BS, :128]
                x_ref[1, r * BS : (r + 1) * BS, lanes] = out[j * BS : (j + 1) * BS, 128:]

    for c in range(2):

        @pl.when(core == c)
        def _():
            at = 0
            for start, end in PARTS[c]:
                q1_ref[at : at + end - start] = x_ref[1, start:end]
                at += end - start
            at = 0
            for start, end in PARTS[1 - c]:
                q3_ref[at : at + end - start] = x_ref[0, start:end]
                at += end - start
            start, end = RESTS[1 - c]
            q2_ref[...] = x_ref[0, start:end]
            start, end = RESTS[c]
            q4_ref[...] = x_ref[1, start:end]


def half_transform(columns, factors, integrals, own, got, swapped):
    aux, rb, kept, bs, _ = integrals.shape
    lanes = aux * 128
    shapes = [(2, rb * bs, lanes)] + [(320, lanes), (192, lanes), (320, lanes), (192, lanes)]
    return pl.pallas_call(
        half_kernel,
        name="half",
        cost_estimate=cost(512 * 1024 * 1024, 8 * 2**20),
        compiler_params=room(8),
        out_shape=[pltpu.VMEM(s, BF16) for s in shapes],
        in_specs=[SMEM] + [VMEM] * 5,
        out_specs=[VMEM] * 5,
        scratch_shapes=[pltpu.VMEM((3 * rb, bs, 256), BF16)],
    )(pltpu.with_memory_space_constraint(columns, pltpu.SMEM), *on_chip(factors, integrals, own, got, swapped))


def nt(a, b):
    return lax.dot_general(a, b, (((1,), (1,)), ((), ())), preferred_element_type=F32)


def own_kernel(x_ref, s_ref, o_ref):
    core = lax.axis_index("aux") % 2
    lane = lax.broadcasted_iota(jnp.int32, (256, x_ref.shape[2]), 1)
    keep = ((lane // OB) % 2 == 1) == (core == 0)

    def picked(ref):
        both = [jnp.concatenate([ref[s:e] for s, e in OWN[c]], axis=0) for c in range(2)]
        return jnp.where(core == 0, both[0], both[1])

    total = None
    for ref, masked in (
        (x_ref.at[0], False), (x_ref.at[1], True), (s_ref.at[1], False), (s_ref.at[0], True),
    ):
        rows = picked(ref)
        if masked:
            rows = jnp.where(keep, rows, jnp.zeros_like(rows))
        part = nt(rows, ref[...])
        total = part if total is None else total + part
    o_ref[...] = total


def own_part(x, s):
    return pl.pallas_call(
        own_kernel,
        name="own",
        cost_estimate=cost(256 * 512 * 2048, 3 * 2**20),
        compiler_params=room(4),
        out_shape=pltpu.VMEM((256, x.shape[1]), F32),
        in_specs=[VMEM] * 2,
        out_specs=VMEM,
    )(*on_chip(x, s))


def place():
    a = lax.axis_index("aux")
    return a // 2, a % 2, jnp.where(a % 2 == 0, 3, 0)


def near_kernel(last, x_ref, s_ref, q1_ref, q3_ref, o_ref, chunks, send_ref):
    d = lax.axis_index("row")
    y, core, _ = place()
    t = nt(q1_ref[...], x_ref[0]) + nt(q3_ref[...], s_ref[1])
    t = jnp.where(d == jnp.where(core == 0, 0, last), 0.0, t)

    @pl.when(core == 0)
    def _():
        chunks[0] = t[:192]
        chunks[1, :128] = t[192:]
        chunks[1, 128:] = o_ref[:64]
        chunks[2] = o_ref[64:]
        chunks[3] = jnp.zeros(chunks.shape[1:], F32)

    @pl.when(core == 1)
    def _():
        chunks[0] = jnp.zeros(chunks.shape[1:], F32)
        chunks[1] = o_ref[:192]
        chunks[2, :64] = o_ref[192:]
        chunks[2, 64:] = t[:128]
        chunks[3] = t[128:]

    send_ref[...] = chunks[y ^ 2].astype(BF16)


def near_part(last, x, s, q1, q3, own):
    return pl.pallas_call(
        functools.partial(near_kernel, last),
        name="near",
        cost_estimate=cost(320 * 512 * 1024, 2 * 2**20),
        compiler_params=room(6),
        out_shape=[pltpu.VMEM((4, 192, x.shape[1]), F32), pltpu.VMEM((192, x.shape[1]), BF16)],
        in_specs=[VMEM] * 5,
        out_specs=[VMEM] * 2,
    )(*on_chip(x, s, q1, q3, own))


def off_kernel(last, x_ref, s_ref, q2_ref, q4_ref, chunks, keep_ref, s1_ref, s3_ref, far_ref):
    d = lax.axis_index("row")
    y, core, far = place()
    u = nt(q2_ref[...], x_ref[1]) + nt(q4_ref[...], s_ref[0])
    u = jnp.where(d == jnp.where(core == 0, last, 0), 0.0, u)
    keep_ref[...] = jnp.where(y == far, u, chunks[y])
    s1_ref[...] = jnp.where(y ^ 1 == far, u, chunks[y ^ 1]).astype(BF16)
    s3_ref[...] = jnp.where(y ^ 3 == far, u, chunks[y ^ 3]).astype(BF16)
    far_ref[...] = u.astype(BF16)


def off_part(last, x, s, q2, q4, near):
    shape = (192, x.shape[1])
    return pl.pallas_call(
        functools.partial(off_kernel, last),
        name="off",
        cost_estimate=cost(192 * 512 * 1024, 4 * 2**20),
        compiler_params=room(4),
        out_shape=[pltpu.VMEM(shape, F32)] + [pltpu.VMEM(shape, BF16)] * 3,
        in_specs=[VMEM] * 5,
        out_specs=[VMEM] * 4,
    )(*on_chip(x, s, q2, q4, near))


def add_kernel(at_far, keep_ref, part_ref, out_ref):
    y, _, far = place()
    out_ref[...] = keep_ref[...] + jnp.where((y == far) == at_far, part_ref[...].astype(F32), 0.0)


def add(name, at_far, kept, part):
    return pl.pallas_call(
        functools.partial(add_kernel, at_far),
        name=name,
        cost_estimate=cost(192 * 512, 2**20),
        compiler_params=room(4),
        out_shape=pltpu.VMEM(kept.shape, F32),
        in_specs=[VMEM] * 2,
        out_specs=VMEM,
    )(*on_chip(kept, part))


def sum_kernel(scale, keep_ref, s1_ref, s3_ref, out_ref):
    total = keep_ref[...] + s1_ref[...].astype(F32) + s3_ref[...].astype(F32)
    out_ref[...] = total * scale


def sum_parts(scale, *parts):
    return pl.pallas_call(
        functools.partial(sum_kernel, scale),
        name="sum",
        cost_estimate=cost(192 * 512, 2**20),
        compiler_params=room(4),
        out_shape=jax.ShapeDtypeStruct(parts[0].shape, F32),
        in_specs=[VMEM] * len(parts),
        out_specs=VMEM,
    )(*on_chip(*parts))


ACROSS = {(y, c): (y ^ 2, c) for y in range(4) for c in range(2)}
FIRST = {**ACROSS, (1, 0): (0, 1), (2, 1): (3, 0)}
FINAL = {
    (1, 0): (3, 0), (2, 1): (0, 1), (0, 0): (1, 1), (3, 1): (2, 0),
    (0, 1): (0, 0), (1, 1): (1, 0), (2, 0): (2, 1), (3, 0): (3, 1),
}


def row_moves(rows, chips, core_0_up, cross):
    pairs = []
    for d in range(rows):
        for y in range(chips):
            for core in range(2):
                step = 1 if (core == 0) == core_0_up else -1
                inside = 0 <= d + step < rows
                target = 1 - core if cross == inside else core
                end = d + step if inside else d
                chip = (y + 1) % chips if cross and not inside else y
                pairs.append(((2 * y + core) * rows + d, (2 * chip + target) * rows + end))
    return pairs


def on_device(integrals, block_columns, orbitals, occ_mask):
    aux_devices, rows = lax.axis_size("aux"), lax.axis_size("row")
    chips = aux_devices // 2
    scale = 1.0 / (integrals.shape[0] * aux_devices * OB) ** 0.5

    def move(value, core_0_up, cross):
        return lax.ppermute(value, ("aux", "row"), row_moves(rows, chips, core_0_up, cross))

    def swap(value):
        return lax.ppermute(value, "aux", [(i, i ^ 1) for i in range(aux_devices)])

    def along_y(value, route):
        pairs = [(2 * y + c, 2 * end[0] + end[1]) for (y, c), end in sorted(route.items())]
        return lax.ppermute(value, "aux", pairs)

    def exchange(value, step):
        return along_y(value, {(y, c): (y ^ step, c) for y in range(chips) for c in range(2)})

    send = halo_to_send(orbitals)
    got = move(send, True, False)
    own, staged, factors, columns = stage(block_columns, occ_mask.T, orbitals, integrals)
    got, own, staged, factors, columns = lax.optimization_barrier(
        (got, own, staged, factors, columns)
    )
    swapped = swap(got)
    x, q1, q2, q3, q4 = half_transform(columns, factors, staged, own, got, swapped)
    r1 = move(q1, True, False)
    r3 = move(q3, False, True)
    others = swap(x)
    r2 = move(q2, False, False)
    r4 = move(q4, True, True)
    o = own_part(x, others)
    near, first = near_part(rows - 1, x, others, r1, r3, o)
    first = along_y(first, FIRST)
    kept, s1, s3, far = off_part(rows - 1, x, others, r2, r4, near)
    kept = add("first", False, kept, first)
    kept = add("far", True, kept, along_y(far, FINAL))
    return sum_parts(scale, kept, exchange(s1, 1), exchange(s3, 3)).T


def solution(mesh):
    in_specs = (P("aux", "row", None, None, None), P("row", None), P("row", None), P())
    out_specs = P("row", "aux")
    return jax.shard_map(
        on_device, mesh=mesh, in_specs=in_specs, out_specs=out_specs, check_vma=False
    )
```

```python
import functools

import jax
import jax.numpy as jnp
from jax import lax
from jax.experimental import pallas as pl
from jax.experimental.pallas import tpu as pltpu
from jax.sharding import PartitionSpec as P

BS = 256
OB = 64
SPLIT = 4
GROUP = 2
BF16 = jnp.bfloat16
F32 = jnp.float32
PARTS = (((0, 192), (384, 512)), ((0, 128), (320, 512)))
RESTS = ((192, 384), (128, 320))
OWN = (((0, 64), (256, 448)), ((64, 256), (448, 512)))
VMEM = pl.BlockSpec(memory_space=pltpu.VMEM)
SMEM = pl.BlockSpec(memory_space=pltpu.SMEM)
ANY = pl.BlockSpec(memory_space=pl.ANY)


def on_chip(*values):
    return [pltpu.with_memory_space_constraint(v, pltpu.VMEM) for v in values]


def in_hbm(value):
    return pltpu.with_memory_space_constraint(value, pltpu.HBM)


def room(megabytes):
    return pltpu.CompilerParams(vmem_limit_bytes=megabytes * 2**20)


def cost(macs, sent):
    return pl.CostEstimate(flops=2 * macs, transcendentals=0, bytes_accessed=sent)


def pair_up(left, right):
    return jnp.concatenate([left[:, OB:], right[:, :OB]], axis=1)


def load_groups(orb_ref, first, buf, sems, parts=1):
    last = orb_ref.shape[1] // 128 - 1
    copies = []
    for j in range(buf.shape[0]):
        group = jnp.clip(first + j, 0, last)
        lanes = pl.ds(pl.multiple_of(group * 128, 128), 128)
        for part in range(parts):
            rows = pl.ds(part * (buf.shape[1] // parts), buf.shape[1] // parts)
            copies.append(
                pltpu.make_async_copy(
                    orb_ref.at[rows, lanes], buf.at[j, rows], sems.at[j * parts + part]
                )
            )
    return copies


def send_kernel(orb_ref, send_ref, buf, sems):
    d = lax.axis_index("row")
    core = lax.axis_index("aux") % 2
    odd = d % 2
    copies = load_groups(orb_ref, (d - 2 - odd) // 2 + 1 - core, buf, sems, SPLIT)
    for copy in copies:
        copy.start()
    for copy in copies:
        copy.wait()
    rows = buf.shape[1]
    half = rows // 2

    @pl.when(odd == 0)
    def _():
        send_ref[:rows] = buf[0]
        send_ref[rows:] = jnp.concatenate([buf[1, :half, :OB], buf[1, half:, :OB]], axis=1)

    @pl.when(odd == 1)
    def _():
        send_ref[:rows] = pair_up(buf[0], buf[1])
        send_ref[rows:] = jnp.concatenate([buf[1, :half, OB:], buf[1, half:, OB:]], axis=1)


def halo_to_send(orbitals):
    rows = orbitals.shape[0]
    return pl.pallas_call(
        send_kernel,
        name="send",
        cost_estimate=cost(512 * 1024, 2**20),
        compiler_params=room(4),
        out_shape=pltpu.VMEM((rows + rows // 2, 128), BF16),
        in_specs=[ANY],
        out_specs=VMEM,
        scratch_shapes=[pltpu.VMEM((2, rows, 128), BF16), pltpu.SemaphoreType.DMA((2 * SPLIT,))],
    )(in_hbm(orbitals))


def stage_kernel(
    cols_hbm, mask_hbm, orb_ref, int_ref, own_ref, near_ref, factor_ref, local_ref,
    cols_ref, mask_ref, buf, sems, int_sems, table_sems,
):
    aux, rb, kept = int_ref.shape[:3]
    loads = [
        pltpu.make_async_copy(int_ref.at[p, r], near_ref.at[p, r], int_sems.at[p, r])
        for p in range(aux)
        for r in range(rb)
    ]
    d = lax.axis_index("row")
    odd = d % 2
    copies = load_groups(orb_ref, (d - 2 - odd) // 2, buf, sems) + loads
    tables = [
        pltpu.make_async_copy(cols_hbm, cols_ref, table_sems.at[0]),
        pltpu.make_async_copy(mask_hbm, mask_ref, table_sems.at[1]),
    ]
    for copy in tables + copies:
        copy.start()
    for copy in tables:
        copy.wait()
    core = lax.axis_index("aux") % 2
    count = mask_ref.shape[0]
    quarter = lax.broadcasted_iota(jnp.int32, (1, 256), 1) // OB
    for r in range(rb):
        factors = []
        for j in range(3):
            s = d - 1 + j
            inside = (s >= 0) & (s < count)
            value = mask_ref[jnp.clip(s, 0, count - 1), rb * d + r]
            factors.append(jnp.where(inside, value, 0).astype(F32))
        low, mid, high = factors
        f0 = jnp.where(core == 0, low, mid)
        f1 = jnp.where(core == 0, mid, high)
        f2 = jnp.where(core == 0, mid, low)
        f3 = jnp.where(core == 0, high, mid)
        factor = jnp.where(
            quarter == 0, f0, jnp.where(quarter == 1, f1, jnp.where(quarter == 2, f2, f3))
        )
        factor_ref[r : r + 1] = factor
        for k in range(kept):
            local_ref[r, k] = cols_ref[r, k] - rb * (d - 1)
    for copy in copies:
        copy.wait()

    @pl.when(odd == 0)
    def _():
        own_ref[:, :128] = pair_up(buf[0], buf[1])
        own_ref[:, 128:] = buf[1]

    @pl.when(odd == 1)
    def _():
        own_ref[:, :128] = buf[1]
        own_ref[:, 128:] = pair_up(buf[1], buf[2])


def stage(block_columns, occ_mask, orbitals, integrals):
    rows, rb = orbitals.shape[0], integrals.shape[1]
    return pl.pallas_call(
        stage_kernel,
        name="stage",
        cost_estimate=cost(512 * 1024, 9 * 2**20),
        compiler_params=room(4),
        out_shape=[
            pltpu.VMEM((rows, 256), BF16),
            pltpu.VMEM(integrals.shape, BF16),
            pltpu.VMEM((rb, 256), F32),
            pltpu.SMEM(block_columns.shape, jnp.int32),
        ],
        in_specs=[ANY] * 4,
        out_specs=[VMEM, VMEM, VMEM, SMEM],
        scratch_shapes=[
            pltpu.SMEM(block_columns.shape, jnp.int32),
            pltpu.SMEM(occ_mask.shape, jnp.int32),
            pltpu.VMEM((3, rows, 128), BF16),
            pltpu.SemaphoreType.DMA((3,)),
            pltpu.SemaphoreType.DMA(integrals.shape[:2]),
            pltpu.SemaphoreType.DMA((2,)),
        ],
    )(*[in_hbm(v) for v in (block_columns, occ_mask, orbitals, integrals)])


def half_kernel(
    cols_ref, factor_ref, int_ref, own_ref, got_ref, swp_ref,
    x_ref, q1_ref, q2_ref, q3_ref, q4_ref, rhs,
):
    core = lax.axis_index("aux") % 2
    aux, rb, kept = int_ref.shape[:3]

    for c in range(2):
        first, second = (slice(0, 128), slice(128, 256))
        if c:
            first, second = second, first

        @pl.when(core == c)
        def _():
            for h in range(rb):
                rows = slice(h * BS, (h + 1) * BS)
                rhs[rb + h, :, :128] = own_ref[rows, first]
                rhs[rb + h, :, 128:] = own_ref[rows, second]
            for j, source in ((0, got_ref if c == 0 else swp_ref), (2, swp_ref if c == 0 else got_ref)):
                for h in range(rb):
                    pair = source[h * BS : (h + 1) * BS]
                    third = source[rb * BS :, h * OB : (h + 1) * OB]
                    rhs[rb * j + h, :, first] = pair
                    rhs[rb * j + h, :, second] = jnp.concatenate([pair[:, OB:], third], axis=1)

    for r in range(rb):
        factor = factor_ref[r : r + 1]
        weights = jnp.concatenate([rhs[cols_ref[r, k]] for k in range(kept)], axis=0)
        for start in range(0, aux, GROUP):
            left = jnp.concatenate(
                [int_ref[start : start + GROUP, r, k].reshape(GROUP * BS, BS) for k in range(kept)], axis=1
            )
            acc = jnp.dot(left, weights, preferred_element_type=F32)
            out = (acc * factor).astype(BF16)
            for j in range(GROUP):
                lanes = slice((start + j) * 128, (start + j + 1) * 128)
                x_ref[0, r * BS : (r + 1) * BS, lanes] = out[j * BS : (j + 1) * BS, :128]
                x_ref[1, r * BS : (r + 1) * BS, lanes] = out[j * BS : (j + 1) * BS, 128:]

    for c in range(2):

        @pl.when(core == c)
        def _():
            at = 0
            for start, end in PARTS[c]:
                q1_ref[at : at + end - start] = x_ref[1, start:end]
                at += end - start
            at = 0
            for start, end in PARTS[1 - c]:
                q3_ref[at : at + end - start] = x_ref[0, start:end]
                at += end - start
            start, end = RESTS[1 - c]
            q2_ref[...] = x_ref[0, start:end]
            start, end = RESTS[c]
            q4_ref[...] = x_ref[1, start:end]


def half_transform(columns, factors, integrals, own, got, swapped):
    aux, rb, kept, bs, _ = integrals.shape
    lanes = aux * 128
    shapes = [(2, rb * bs, lanes)] + [(320, lanes), (192, lanes), (320, lanes), (192, lanes)]
    return pl.pallas_call(
        half_kernel,
        name="half",
        cost_estimate=cost(512 * 1024 * 1024, 8 * 2**20),
        compiler_params=room(8),
        out_shape=[pltpu.VMEM(s, BF16) for s in shapes],
        in_specs=[SMEM] + [VMEM] * 5,
        out_specs=[VMEM] * 5,
        scratch_shapes=[pltpu.VMEM((3 * rb, bs, 256), BF16)],
    )(pltpu.with_memory_space_constraint(columns, pltpu.SMEM), *on_chip(factors, integrals, own, got, swapped))


def nt(a, b):
    return lax.dot_general(a, b, (((1,), (1,)), ((), ())), preferred_element_type=F32)


def own_kernel(x_ref, s_ref, o_ref):
    core = lax.axis_index("aux") % 2
    lane = lax.broadcasted_iota(jnp.int32, (256, x_ref.shape[2]), 1)
    keep = ((lane // OB) % 2 == 1) == (core == 0)

    def picked(ref):
        both = [jnp.concatenate([ref[s:e] for s, e in OWN[c]], axis=0) for c in range(2)]
        return jnp.where(core == 0, both[0], both[1])

    total = None
    for ref, masked in (
        (x_ref.at[0], False), (x_ref.at[1], True), (s_ref.at[1], False), (s_ref.at[0], True),
    ):
        rows = picked(ref)
        if masked:
            rows = jnp.where(keep, rows, jnp.zeros_like(rows))
        part = nt(rows, ref[...])
        total = part if total is None else total + part
    o_ref[...] = total


def own_part(x, s):
    return pl.pallas_call(
        own_kernel,
        name="own",
        cost_estimate=cost(256 * 512 * 2048, 3 * 2**20),
        compiler_params=room(4),
        out_shape=pltpu.VMEM((256, x.shape[1]), F32),
        in_specs=[VMEM] * 2,
        out_specs=VMEM,
    )(*on_chip(x, s))


def place():
    a = lax.axis_index("aux")
    return a // 2, a % 2, jnp.where(a % 2 == 0, 3, 0)


def near_kernel(last, x_ref, s_ref, q3_ref, q1_ref, o_ref, chunks, send_ref):
    d = lax.axis_index("row")
    y, core, _ = place()
    t = nt(q1_ref[...], x_ref[0]) + nt(q3_ref[...], s_ref[1])
    t = jnp.where(d == jnp.where(core == 0, 0, last), 0.0, t)

    @pl.when(core == 0)
    def _():
        chunks[0] = t[:192]
        chunks[1, :128] = t[192:]
        chunks[1, 128:] = o_ref[:64]
        chunks[2] = o_ref[64:]
        chunks[3] = jnp.zeros(chunks.shape[1:], F32)

    @pl.when(core == 1)
    def _():
        chunks[0] = jnp.zeros(chunks.shape[1:], F32)
        chunks[1] = o_ref[:192]
        chunks[2, :64] = o_ref[192:]
        chunks[2, 64:] = t[:128]
        chunks[3] = t[128:]

    send_ref[...] = chunks[y ^ 2].astype(BF16)


def near_part(last, x, s, q3, q1, own):
    return pl.pallas_call(
        functools.partial(near_kernel, last),
        name="near",
        cost_estimate=cost(320 * 512 * 1024, 2 * 2**20),
        compiler_params=room(6),
        out_shape=[pltpu.VMEM((4, 192, x.shape[1]), F32), pltpu.VMEM((192, x.shape[1]), BF16)],
        in_specs=[VMEM] * 5,
        out_specs=[VMEM] * 2,
    )(*on_chip(x, s, q3, q1, own))


def off_kernel(last, x_ref, s_ref, q4_ref, q2_ref, chunks, keep_ref, s1_ref, s3_ref, far_ref):
    d = lax.axis_index("row")
    y, core, far = place()
    u = nt(q2_ref[...], x_ref[1]) + nt(q4_ref[...], s_ref[0])
    u = jnp.where(d == jnp.where(core == 0, last, 0), 0.0, u)
    keep_ref[...] = jnp.where(y == far, u, chunks[y])
    s1_ref[...] = jnp.where(y ^ 1 == far, u, chunks[y ^ 1]).astype(BF16)
    s3_ref[...] = jnp.where(y ^ 3 == far, u, chunks[y ^ 3]).astype(BF16)
    far_ref[...] = u.astype(BF16)


def off_part(last, x, s, q4, q2, near):
    shape = (192, x.shape[1])
    return pl.pallas_call(
        functools.partial(off_kernel, last),
        name="off",
        cost_estimate=cost(192 * 512 * 1024, 4 * 2**20),
        compiler_params=room(4),
        out_shape=[pltpu.VMEM(shape, F32)] + [pltpu.VMEM(shape, BF16)] * 3,
        in_specs=[VMEM] * 5,
        out_specs=[VMEM] * 4,
    )(*on_chip(x, s, q4, q2, near))


def add_kernel(at_far, keep_ref, part_ref, out_ref):
    y, _, far = place()
    out_ref[...] = keep_ref[...] + jnp.where((y == far) == at_far, part_ref[...].astype(F32), 0.0)


def add(name, at_far, kept, part):
    return pl.pallas_call(
        functools.partial(add_kernel, at_far),
        name=name,
        cost_estimate=cost(192 * 512, 2**20),
        compiler_params=room(4),
        out_shape=pltpu.VMEM(kept.shape, F32),
        in_specs=[VMEM] * 2,
        out_specs=VMEM,
    )(*on_chip(kept, part))


def sum_kernel(scale, keep_ref, s1_ref, s3_ref, out_ref):
    total = keep_ref[...] + s1_ref[...].astype(F32) + s3_ref[...].astype(F32)
    out_ref[...] = total * scale


def sum_parts(scale, *parts):
    return pl.pallas_call(
        functools.partial(sum_kernel, scale),
        name="sum",
        cost_estimate=cost(192 * 512, 2**20),
        compiler_params=room(4),
        out_shape=jax.ShapeDtypeStruct(parts[0].shape, F32),
        in_specs=[VMEM] * len(parts),
        out_specs=VMEM,
    )(*on_chip(*parts))


ACROSS = {(y, c): (y ^ 2, c) for y in range(4) for c in range(2)}
FIRST = {**ACROSS, (1, 0): (0, 1), (2, 1): (3, 0)}
FINAL = {
    (1, 0): (3, 0), (2, 1): (0, 1), (0, 0): (1, 1), (3, 1): (2, 0),
    (0, 1): (0, 0), (1, 1): (1, 0), (2, 0): (2, 1), (3, 0): (3, 1),
}


def row_moves(rows, chips, core_0_up, cross):
    pairs = []
    for d in range(rows):
        for y in range(chips):
            for core in range(2):
                step = 1 if (core == 0) == core_0_up else -1
                inside = 0 <= d + step < rows
                target = 1 - core if cross == inside else core
                end = d + step if inside else d
                chip = (y + 1) % chips if cross and not inside else y
                pairs.append(((2 * y + core) * rows + d, (2 * chip + target) * rows + end))
    return pairs


def on_device(integrals, block_columns, orbitals, occ_mask):
    aux_devices, rows = lax.axis_size("aux"), lax.axis_size("row")
    chips = aux_devices // 2
    scale = 1.0 / (integrals.shape[0] * aux_devices * OB) ** 0.5

    def move(value, core_0_up, cross):
        return lax.ppermute(value, ("aux", "row"), row_moves(rows, chips, core_0_up, cross))

    def swap(value):
        return lax.ppermute(value, "aux", [(i, i ^ 1) for i in range(aux_devices)])

    def along_y(value, route):
        pairs = [(2 * y + c, 2 * end[0] + end[1]) for (y, c), end in sorted(route.items())]
        return lax.ppermute(value, "aux", pairs)

    def exchange(value, step):
        return along_y(value, {(y, c): (y ^ step, c) for y in range(chips) for c in range(2)})

    send = halo_to_send(orbitals)
    got = move(send, True, False)
    own, staged, factors, columns = stage(block_columns, occ_mask.T, orbitals, integrals)
    got, own, staged, factors, columns = lax.optimization_barrier(
        (got, own, staged, factors, columns)
    )
    swapped = swap(got)
    x, q1, q2, q3, q4 = half_transform(columns, factors, staged, own, got, swapped)
    r1 = move(q1, True, False)
    r3 = move(q3, False, True)
    others = swap(x)
    r2 = move(q2, False, False)
    r4 = move(q4, True, True)
    o = own_part(x, others)
    near, first = near_part(rows - 1, x, others, r3, r1, o)
    first = along_y(first, FIRST)
    kept, s1, s3, far = off_part(rows - 1, x, others, r4, r2, near)
    kept = add("first", False, kept, first)
    kept = add("far", True, kept, along_y(far, FINAL))
    return sum_parts(scale, kept, exchange(s1, 1), exchange(s3, 3)).T


def solution(mesh):
    in_specs = (P("aux", "row", None, None, None), P("row", None), P("row", None), P())
    out_specs = P("row", "aux")
    return jax.shard_map(
        on_device, mesh=mesh, in_specs=in_specs, out_specs=out_specs, check_vma=False
    )
```

```python
import functools

import jax
import jax.numpy as jnp
from jax import lax
from jax.experimental import pallas as pl
from jax.experimental.pallas import tpu as pltpu
from jax.sharding import PartitionSpec as P

BS = 256
OB = 64
SPLIT = 4
GROUP = 2
BF16 = jnp.bfloat16
F32 = jnp.float32
PARTS = (((0, 192), (384, 512)), ((0, 128), (320, 512)))
RESTS = ((192, 384), (128, 320))
OWN = (((0, 64), (256, 448)), ((64, 256), (448, 512)))
VMEM = pl.BlockSpec(memory_space=pltpu.VMEM)
SMEM = pl.BlockSpec(memory_space=pltpu.SMEM)
ANY = pl.BlockSpec(memory_space=pl.ANY)


def on_chip(*values):
    return [pltpu.with_memory_space_constraint(v, pltpu.VMEM) for v in values]


def in_hbm(value):
    return pltpu.with_memory_space_constraint(value, pltpu.HBM)


def room(megabytes):
    return pltpu.CompilerParams(vmem_limit_bytes=megabytes * 2**20)


def cost(macs, sent):
    return pl.CostEstimate(flops=2 * macs, transcendentals=0, bytes_accessed=sent)


def pair_up(left, right):
    return jnp.concatenate([left[:, OB:], right[:, :OB]], axis=1)


def load_groups(orb_ref, first, buf, sems, parts=1):
    last = orb_ref.shape[1] // 128 - 1
    copies = []
    for j in range(buf.shape[0]):
        group = jnp.clip(first + j, 0, last)
        lanes = pl.ds(pl.multiple_of(group * 128, 128), 128)
        for part in range(parts):
            rows = pl.ds(part * (buf.shape[1] // parts), buf.shape[1] // parts)
            copies.append(
                pltpu.make_async_copy(
                    orb_ref.at[rows, lanes], buf.at[j, rows], sems.at[j * parts + part]
                )
            )
    return copies


def send_kernel(orb_ref, send_ref, buf, sems):
    d = lax.axis_index("row")
    core = lax.axis_index("aux") % 2
    odd = d % 2
    copies = load_groups(orb_ref, (d - 2 - odd) // 2 + 1 - core, buf, sems, SPLIT)
    for copy in copies:
        copy.start()
    for copy in copies:
        copy.wait()
    rows = buf.shape[1]
    half = rows // 2

    @pl.when(odd == 0)
    def _():
        send_ref[:rows] = buf[0]
        send_ref[rows:] = jnp.concatenate([buf[1, :half, :OB], buf[1, half:, :OB]], axis=1)

    @pl.when(odd == 1)
    def _():
        send_ref[:rows] = pair_up(buf[0], buf[1])
        send_ref[rows:] = jnp.concatenate([buf[1, :half, OB:], buf[1, half:, OB:]], axis=1)


def halo_to_send(orbitals):
    rows = orbitals.shape[0]
    return pl.pallas_call(
        send_kernel,
        name="send",
        cost_estimate=cost(512 * 1024, 2**20),
        compiler_params=room(4),
        out_shape=pltpu.VMEM((rows + rows // 2, 128), BF16),
        in_specs=[ANY],
        out_specs=VMEM,
        scratch_shapes=[pltpu.VMEM((2, rows, 128), BF16), pltpu.SemaphoreType.DMA((2 * SPLIT,))],
    )(in_hbm(orbitals))


def stage_kernel(
    cols_hbm, mask_hbm, orb_ref, int_ref, own_ref, near_ref, factor_ref, local_ref,
    cols_ref, mask_ref, buf, sems, int_sems, table_sems,
):
    aux, rb, kept = int_ref.shape[:3]
    loads = [
        pltpu.make_async_copy(int_ref.at[p, r], near_ref.at[p, r], int_sems.at[p, r])
        for p in range(aux)
        for r in range(rb)
    ]
    d = lax.axis_index("row")
    odd = d % 2
    copies = load_groups(orb_ref, (d - 2 - odd) // 2, buf, sems) + loads
    tables = [
        pltpu.make_async_copy(cols_hbm, cols_ref, table_sems.at[0]),
        pltpu.make_async_copy(mask_hbm, mask_ref, table_sems.at[1]),
    ]
    for copy in tables + copies:
        copy.start()
    for copy in tables:
        copy.wait()
    core = lax.axis_index("aux") % 2
    count = mask_ref.shape[0]
    quarter = lax.broadcasted_iota(jnp.int32, (1, 256), 1) // OB
    for r in range(rb):
        factors = []
        for j in range(3):
            s = d - 1 + j
            inside = (s >= 0) & (s < count)
            value = mask_ref[jnp.clip(s, 0, count - 1), rb * d + r]
            factors.append(jnp.where(inside, value, 0).astype(F32))
        low, mid, high = factors
        f0 = jnp.where(core == 0, low, mid)
        f1 = jnp.where(core == 0, mid, high)
        f2 = jnp.where(core == 0, mid, low)
        f3 = jnp.where(core == 0, high, mid)
        factor = jnp.where(
            quarter == 0, f0, jnp.where(quarter == 1, f1, jnp.where(quarter == 2, f2, f3))
        )
        factor_ref[r : r + 1] = factor
        for k in range(kept):
            local_ref[r, k] = cols_ref[r, k] - rb * (d - 1)
    for copy in copies:
        copy.wait()

    @pl.when(odd == 0)
    def _():
        own_ref[:, :128] = pair_up(buf[0], buf[1])
        own_ref[:, 128:] = buf[1]

    @pl.when(odd == 1)
    def _():
        own_ref[:, :128] = buf[1]
        own_ref[:, 128:] = pair_up(buf[1], buf[2])


def stage(block_columns, occ_mask, orbitals, integrals):
    rows, rb = orbitals.shape[0], integrals.shape[1]
    return pl.pallas_call(
        stage_kernel,
        name="stage",
        cost_estimate=cost(512 * 1024, 9 * 2**20),
        compiler_params=room(4),
        out_shape=[
            pltpu.VMEM((rows, 256), BF16),
            pltpu.VMEM(integrals.shape, BF16),
            pltpu.VMEM((rb, 256), F32),
            pltpu.SMEM(block_columns.shape, jnp.int32),
        ],
        in_specs=[ANY] * 4,
        out_specs=[VMEM, VMEM, VMEM, SMEM],
        scratch_shapes=[
            pltpu.SMEM(block_columns.shape, jnp.int32),
            pltpu.SMEM(occ_mask.shape, jnp.int32),
            pltpu.VMEM((3, rows, 128), BF16),
            pltpu.SemaphoreType.DMA((3,)),
            pltpu.SemaphoreType.DMA(integrals.shape[:2]),
            pltpu.SemaphoreType.DMA((2,)),
        ],
    )(*[in_hbm(v) for v in (block_columns, occ_mask, orbitals, integrals)])


def half_kernel(
    cols_ref, factor_ref, int_ref, own_ref, got_ref, swp_ref,
    x_ref, q1_ref, q2_ref, q3_ref, q4_ref, rhs,
):
    core = lax.axis_index("aux") % 2
    aux, rb, kept = int_ref.shape[:3]

    for c in range(2):
        first, second = (slice(0, 128), slice(128, 256))
        if c:
            first, second = second, first

        @pl.when(core == c)
        def _():
            for h in range(rb):
                rows = slice(h * BS, (h + 1) * BS)
                rhs[rb + h, :, :128] = own_ref[rows, first]
                rhs[rb + h, :, 128:] = own_ref[rows, second]
            for j, source in ((0, got_ref if c == 0 else swp_ref), (2, swp_ref if c == 0 else got_ref)):
                for h in range(rb):
                    pair = source[h * BS : (h + 1) * BS]
                    third = source[rb * BS :, h * OB : (h + 1) * OB]
                    rhs[rb * j + h, :, first] = pair
                    rhs[rb * j + h, :, second] = jnp.concatenate([pair[:, OB:], third], axis=1)

    for r in range(rb):
        factor = factor_ref[r : r + 1]
        weights = jnp.concatenate([rhs[cols_ref[r, k]] for k in range(kept)], axis=0)
        for start in range(0, aux, GROUP):
            left = jnp.concatenate(
                [int_ref[start : start + GROUP, r, k].reshape(GROUP * BS, BS) for k in range(kept)], axis=1
            )
            acc = jnp.dot(left, weights, preferred_element_type=F32)
            out = (acc * factor).astype(BF16)
            for j in range(GROUP):
                lanes = slice((start + j) * 128, (start + j + 1) * 128)
                x_ref[0, r * BS : (r + 1) * BS, lanes] = out[j * BS : (j + 1) * BS, :128]
                x_ref[1, r * BS : (r + 1) * BS, lanes] = out[j * BS : (j + 1) * BS, 128:]

    for c in range(2):

        @pl.when(core == c)
        def _():
            at = 0
            for start, end in PARTS[c]:
                q1_ref[at : at + end - start] = x_ref[1, start:end]
                at += end - start
            at = 0
            for start, end in PARTS[1 - c]:
                q3_ref[at : at + end - start] = x_ref[0, start:end]
                at += end - start
            start, end = RESTS[1 - c]
            q2_ref[...] = x_ref[0, start:end]
            start, end = RESTS[c]
            q4_ref[...] = x_ref[1, start:end]


def half_transform(columns, factors, integrals, own, got, swapped):
    aux, rb, kept, bs, _ = integrals.shape
    lanes = aux * 128
    shapes = [(2, rb * bs, lanes)] + [(320, lanes), (192, lanes), (320, lanes), (192, lanes)]
    return pl.pallas_call(
        half_kernel,
        name="half",
        cost_estimate=cost(512 * 1024 * 1024, 8 * 2**20),
        compiler_params=room(8),
        out_shape=[pltpu.VMEM(s, BF16) for s in shapes],
        in_specs=[SMEM] + [VMEM] * 5,
        out_specs=[VMEM] * 5,
        scratch_shapes=[pltpu.VMEM((3 * rb, bs, 256), BF16)],
    )(pltpu.with_memory_space_constraint(columns, pltpu.SMEM), *on_chip(factors, integrals, own, got, swapped))


def nt(a, b):
    return lax.dot_general(a, b, (((1,), (1,)), ((), ())), preferred_element_type=F32)


def own_kernel(x_ref, s_ref, o_ref):
    core = lax.axis_index("aux") % 2
    lane = lax.broadcasted_iota(jnp.int32, (256, x_ref.shape[2]), 1)
    keep = ((lane // OB) % 2 == 1) == (core == 0)

    def picked(ref):
        both = [jnp.concatenate([ref[s:e] for s, e in OWN[c]], axis=0) for c in range(2)]
        return jnp.where(core == 0, both[0], both[1])

    total = None
    for ref, masked in (
        (x_ref.at[0], False), (x_ref.at[1], True), (s_ref.at[1], False), (s_ref.at[0], True),
    ):
        rows = picked(ref)
        if masked:
            rows = jnp.where(keep, rows, jnp.zeros_like(rows))
        part = nt(rows, ref[...])
        total = part if total is None else total + part
    o_ref[...] = total


def own_part(x, s):
    return pl.pallas_call(
        own_kernel,
        name="own",
        cost_estimate=cost(256 * 512 * 2048, 3 * 2**20),
        compiler_params=room(4),
        out_shape=pltpu.VMEM((256, x.shape[1]), F32),
        in_specs=[VMEM] * 2,
        out_specs=VMEM,
    )(*on_chip(x, s))


def place():
    a = lax.axis_index("aux")
    return a // 2, a % 2, jnp.where(a % 2 == 0, 3, 0)


def near_kernel(last, x_ref, s_ref, q3_ref, q1_ref, o_ref, chunks, send_ref):
    d = lax.axis_index("row")
    y, core, _ = place()
    t = nt(q1_ref[...], x_ref[0]) + nt(q3_ref[...], s_ref[1])
    t = jnp.where(d == jnp.where(core == 0, 0, last), 0.0, t)

    @pl.when(core == 0)
    def _():
        chunks[0] = t[:192]
        chunks[1, :128] = t[192:]
        chunks[1, 128:] = o_ref[:64]
        chunks[2] = o_ref[64:]
        chunks[3] = jnp.zeros(chunks.shape[1:], F32)

    @pl.when(core == 1)
    def _():
        chunks[0] = jnp.zeros(chunks.shape[1:], F32)
        chunks[1] = o_ref[:192]
        chunks[2, :64] = o_ref[192:]
        chunks[2, 64:] = t[:128]
        chunks[3] = t[128:]

    send_ref[...] = chunks[y ^ 2].astype(BF16)


def near_part(last, x, s, q3, q1, own):
    return pl.pallas_call(
        functools.partial(near_kernel, last),
        name="near",
        cost_estimate=cost(320 * 512 * 1024, 2 * 2**20),
        compiler_params=room(6),
        out_shape=[pltpu.VMEM((4, 192, x.shape[1]), F32), pltpu.VMEM((192, x.shape[1]), BF16)],
        in_specs=[VMEM] * 5,
        out_specs=[VMEM] * 2,
    )(*on_chip(x, s, q3, q1, own))


def off_kernel(last, x_ref, s_ref, q4_ref, q2_ref, chunks, keep_ref, s1_ref, s3_ref, far_ref):
    d = lax.axis_index("row")
    y, core, far = place()
    u = nt(q2_ref[...], x_ref[1]) + nt(q4_ref[...], s_ref[0])
    u = jnp.where(d == jnp.where(core == 0, last, 0), 0.0, u)
    keep_ref[...] = jnp.where(y == far, u, chunks[y])
    s1_ref[...] = jnp.where(y ^ 1 == far, u, chunks[y ^ 1]).astype(BF16)
    s3_ref[...] = jnp.where(y ^ 3 == far, u, chunks[y ^ 3]).astype(BF16)
    far_ref[...] = u.astype(BF16)


def off_part(last, x, s, q4, q2, near):
    shape = (192, x.shape[1])
    return pl.pallas_call(
        functools.partial(off_kernel, last),
        name="off",
        cost_estimate=cost(192 * 512 * 1024, 4 * 2**20),
        compiler_params=room(4),
        out_shape=[pltpu.VMEM(shape, F32)] + [pltpu.VMEM(shape, BF16)] * 3,
        in_specs=[VMEM] * 5,
        out_specs=[VMEM] * 4,
    )(*on_chip(x, s, q4, q2, near))


def add_kernel(at_far, keep_ref, part_ref, out_ref):
    y, _, far = place()
    out_ref[...] = keep_ref[...] + jnp.where((y == far) == at_far, part_ref[...].astype(F32), 0.0)


def add(name, at_far, kept, part):
    return pl.pallas_call(
        functools.partial(add_kernel, at_far),
        name=name,
        cost_estimate=cost(192 * 512, 2**20),
        compiler_params=room(4),
        out_shape=pltpu.VMEM(kept.shape, F32),
        in_specs=[VMEM] * 2,
        out_specs=VMEM,
    )(*on_chip(kept, part))


def sum_kernel(scale, keep_ref, s1_ref, s3_ref, out_ref, buf, sems):
    pieces = sems.shape[0]
    rows = buf.shape[0] // pieces
    copies = []
    for i in range(pieces):
        at = pl.ds(i * rows, rows)
        total = keep_ref[at] + s1_ref[at].astype(F32) + s3_ref[at].astype(F32)
        buf[at] = total * scale
        copies.append(pltpu.make_async_copy(buf.at[at], out_ref.at[at], sems.at[i]))
        copies[-1].start()
    for copy in copies:
        copy.wait()


def sum_parts(scale, *parts):
    shape = parts[0].shape
    return pl.pallas_call(
        functools.partial(sum_kernel, scale),
        name="sum",
        cost_estimate=cost(192 * 512, 2**20),
        compiler_params=room(4),
        out_shape=jax.ShapeDtypeStruct(shape, F32),
        in_specs=[VMEM] * len(parts),
        out_specs=ANY,
        scratch_shapes=[pltpu.VMEM(shape, F32), pltpu.SemaphoreType.DMA((6,))],
    )(*on_chip(*parts))


ACROSS = {(y, c): (y ^ 2, c) for y in range(4) for c in range(2)}
FIRST = {**ACROSS, (1, 0): (0, 1), (2, 1): (3, 0)}
FINAL = {
    (1, 0): (3, 0), (2, 1): (0, 1), (0, 0): (1, 1), (3, 1): (2, 0),
    (0, 1): (0, 0), (1, 1): (1, 0), (2, 0): (2, 1), (3, 0): (3, 1),
}


def row_moves(rows, chips, core_0_up, cross):
    pairs = []
    for d in range(rows):
        for y in range(chips):
            for core in range(2):
                step = 1 if (core == 0) == core_0_up else -1
                inside = 0 <= d + step < rows
                target = 1 - core if cross == inside else core
                end = d + step if inside else d
                chip = (y + 1) % chips if cross and not inside else y
                pairs.append(((2 * y + core) * rows + d, (2 * chip + target) * rows + end))
    return pairs


def on_device(integrals, block_columns, orbitals, occ_mask):
    aux_devices, rows = lax.axis_size("aux"), lax.axis_size("row")
    chips = aux_devices // 2
    scale = 1.0 / (integrals.shape[0] * aux_devices * OB) ** 0.5

    def move(value, core_0_up, cross):
        return lax.ppermute(value, ("aux", "row"), row_moves(rows, chips, core_0_up, cross))

    def swap(value):
        return lax.ppermute(value, "aux", [(i, i ^ 1) for i in range(aux_devices)])

    def along_y(value, route):
        pairs = [(2 * y + c, 2 * end[0] + end[1]) for (y, c), end in sorted(route.items())]
        return lax.ppermute(value, "aux", pairs)

    def exchange(value, step):
        return along_y(value, {(y, c): (y ^ step, c) for y in range(chips) for c in range(2)})

    send = halo_to_send(orbitals)
    got = move(send, True, False)
    own, staged, factors, columns = stage(block_columns, occ_mask.T, orbitals, integrals)
    got, own, staged, factors, columns = lax.optimization_barrier(
        (got, own, staged, factors, columns)
    )
    swapped = swap(got)
    x, q1, q2, q3, q4 = half_transform(columns, factors, staged, own, got, swapped)
    r1 = move(q1, True, False)
    r3 = move(q3, False, True)
    others = swap(x)
    r2 = move(q2, False, False)
    r4 = move(q4, True, True)
    o = own_part(x, others)
    near, first = near_part(rows - 1, x, others, r3, r1, o)
    first = along_y(first, FIRST)
    kept, s1, s3, far = off_part(rows - 1, x, others, r4, r2, near)
    kept = add("first", False, kept, first)
    kept = add("far", True, kept, along_y(far, FINAL))
    return sum_parts(scale, kept, exchange(s1, 1), exchange(s3, 3)).T


def solution(mesh):
    in_specs = (P("aux", "row", None, None, None), P("row", None), P("row", None), P())
    out_specs = P("row", "aux")
    return jax.shard_map(
        on_device, mesh=mesh, in_specs=in_specs, out_specs=out_specs, check_vma=False
    )
```
